32 devices in a mesh: depth: 8 (over z, y), space: 4 (over x, core).
Axes of the slice: x: 2, y: 2, z: 4, core: 2. Of those that a mesh axis runs over, the one named last changes fastest.
Arguments:
- coarse_states: float32 [8, 32, 128, 128], P('depth', 'space'), may hold values from -6 to 6
- first_kernels: bfloat16 [32, 9, 128, 128], P('depth'), may hold values from -0.1875 to 0.1875
- second_kernels: bfloat16 [32, 9, 128, 128], P('depth'), may hold values from -0.1875 to 0.1875
- coarse_channel_gain: float32 [8, 128], replicated, may hold values from 0 to 1, as said below
Outputs:
- states: float32 [32, 32, 128, 128], P('depth', 'space')
- relaxed: float32 [8, 32, 128, 128], P('depth', 'space')
The draws below stay inside these ranges and needn't reach their ends.
Inputs may be any that keep to these rules, and one draw needn't show every extreme that they name: `coarse_channel_gain`: each entry is positive and at most 1.
All inputs are finite; a program needn't handle non-finite values.
Results may differ from the reference program's by a relative error of at most 0.01.
Values may be sent and summed in bfloat16 or wider, within the bound.
A program may use at most 128 MiB of HBM per device.

```python
import jax
import jax.numpy as jnp
from jax import lax

C = 128
CF = 4
W = 128
COARSE_POINTS = 8
LAYERS = 32
H = 32


def draw_coarse_channel_gain(key, part):
    random_keys = [jax.random.fold_in(key, 101 + index) for index in range(7)]
    share = 0.5
    slow = jax.random.uniform(random_keys[0], (C,)) < share
    slow_rate = jnp.log(0.2) / COARSE_POINTS * jax.random.uniform(random_keys[1], (C,), jnp.float32, 0.3, 1.0)
    fast_rate = jnp.log(0.1) / jax.random.uniform(random_keys[2], (C,), jnp.float32, 4.0, 20.0)
    rate = jnp.where(slow, slow_rate, fast_rate)
    jitter = jax.random.uniform(random_keys[3], (COARSE_POINTS, 1), jnp.float32, 0.5, 1.5)
    relaxation_sweep = jax.random.uniform(random_keys[4], (COARSE_POINTS, 1)) < 3.0 / COARSE_POINTS
    multiplier = jnp.where(relaxation_sweep, jax.random.uniform(random_keys[5], (COARSE_POINTS, 1), jnp.float32, 0.5, 0.8), 1.0)
    return (jnp.exp(rate[None, :] * jitter) * multiplier).astype(jnp.float32)


def shard_levels(stream_key, extent, shards, low, high):
    loudness, own = 1.0, jax.random.fold_in(stream_key, 6)
    for axis_at, blocks in shards:
        heights = jnp.exp(jax.random.uniform(jax.random.fold_in(own, axis_at), (blocks,), jnp.float32, low / len(shards), high / len(shards)))
        loudness = loudness * jnp.repeat(heights, extent[axis_at] // blocks).reshape([-1 if axis == axis_at else 1 for axis in range(len(extent))])
    return loudness


def gaussian(stream_key, extent, scale, most, cuts=(), kind=jnp.bfloat16):
    values = jax.random.normal(stream_key, extent, jnp.float32) * scale
    if len(cuts) > 0:
        values = shard_levels(stream_key, extent, cuts, -0.22, 0.18) * values
    return jnp.clip(values, min=-most, max=most).astype(kind)


def setup_inputs(seed: int = 0) -> dict:
    streams_of = jax.random.split(jax.random.key(seed), 5)
    return {
        "coarse_states": gaussian(streams_of[0], (COARSE_POINTS, H, W, C), 1.0, 6.0, ((0, 8), (1, 4)), jnp.float32),
        "first_kernels": gaussian(streams_of[1], (LAYERS, 9, C, C), (9 * C) ** -0.5, 0.1875, ((0, 8),)),
        "second_kernels": gaussian(streams_of[2], (LAYERS, 9, C, C), (9 * C) ** -0.5, 0.1875, ((0, 8),)),
        "coarse_channel_gain": draw_coarse_channel_gain(jax.random.fold_in(streams_of[4], 71), 0),
    }


def conv_taps(padded, kernel):
    rows = padded.shape[0] - 2
    cols = padded.shape[1]
    wide = jnp.pad(padded, ((0, 0), (1, 1), (0, 0)))
    parts = [wide[a:a + rows, b:b + cols, :] for a in range(3) for b in range(3)]
    stacked = jnp.concatenate(parts, axis=-1).reshape(rows * cols, -1)
    flat = kernel.reshape(-1, kernel.shape[-1])
    return jnp.dot(stacked, flat, preferred_element_type=jnp.float32).reshape(rows, cols, -1)


def layer_step(state, first, second_half):
    inner = jnp.pad(state.astype(jnp.bfloat16), ((1, 1), (0, 0), (0, 0)))
    hidden = jnp.tanh(conv_taps(inner, first)).astype(jnp.bfloat16)
    outer = conv_taps(jnp.pad(hidden, ((1, 1), (0, 0), (0, 0))), second_half)
    return state + 0.5 * jnp.tanh(outer)


def propagate(start, firsts, seconds):
    state = start
    for index in range(CF):
        state = layer_step(state, firsts[index], seconds[index])
    return state


def reference(coarse_states, first_kernels, second_kernels, coarse_channel_gain):
    firsts = first_kernels.reshape(COARSE_POINTS, CF, 9, C, C)
    seconds = second_kernels.reshape(COARSE_POINTS, CF, 9, C, C)

    def sweep_all(starts):
        return lax.map(lambda args: propagate(args[0], args[1], args[2]), (starts, firsts, seconds))

    y_first = sweep_all(coarse_states)
    c_first = jnp.concatenate([coarse_states[:1], y_first[:-1]], axis=0)
    y_second = sweep_all(c_first)
    resid = jnp.concatenate([jnp.zeros_like(c_first[:1]), y_second[:-1] - c_first[1:]], axis=0)

    def chain(carry, pair):
        gain, term = pair
        nxt = gain * carry + term
        return nxt, nxt

    zero_state = jnp.zeros(coarse_states.shape[1:], jnp.float32)
    _, errors = lax.scan(chain, zero_state, (coarse_channel_gain, resid))
    c_second = c_first + errors

    def points(args):
        state, fk, sk = args
        listing = [state]
        for index in range(CF - 1):
            state = layer_step(state, fk[index], sk[index])
            listing.append(state)
        return jnp.stack(listing, axis=0)

    result = lax.map(points, (c_second, firsts, seconds))
    return result.reshape(LAYERS, H, W, C), y_second
```

```python
import functools

import jax
import jax.numpy as jnp
from jax import lax
from jax.experimental import pallas as pl
from jax.experimental.pallas import tpu as pltpu
from jax.sharding import PartitionSpec as P

MESH = pl.DeviceIdType.MESH
F32 = jnp.float32
BF16 = jnp.bfloat16


def pair_weight(tap, none):
    blocks = []
    for i in range(4):
        for b in range(3):
            one = tap(i, b) if i < 3 else none
            two = tap(i - 1, b) if i > 0 else none
            blocks.append(jnp.concatenate([one, two], axis=1))
    return jnp.concatenate(blocks, axis=0)


def cycle_kernel(
    depths,
    spaces,
    start_ref,
    first_ref,
    second_ref,
    gain_ref,
    states_ref,
    relaxed_ref,
    wf,
    ws,
    gains,
    X,
    S,
    own,
    pair_in,
    edge_in,
    ybuf,
    qsend,
    qrecv,
    tsend,
    trecv,
    fsend,
    frecv,
    start_sem,
    weight_sem,
    gain_sem,
    pair_send,
    pair_recv,
    edge_send,
    edge_recv,
    y_send,
    y_recv,
    scan_send,
    scan_recv,
    out_sem,
    relaxed_sem,
):
    layers = first_ref.shape[0]
    rows, cols, chans = start_ref.shape
    convs = 2 * layers
    far = 2 * rows
    half = rows // 2
    d = lax.axis_index("depth")
    s = lax.axis_index("space")
    odd = d % 2
    partner = d + 1 - 2 * odd
    flip = 1 - s % 2
    pair = s + 1 - 2 * (s % 2)
    across = s - 1 + 2 * (s % 2)
    inside = (across >= 0) & (across < spaces)

    def image_row(r):
        return r + flip * (rows - 1 - 2 * r)

    def start_copy(r):
        return pltpu.make_async_copy(
            start_ref.at[image_row(r)], S.at[0, rows + r], start_sem.at[r]
        )

    def weight_copy(n, l):
        src, dst = ((first_ref, wf), (second_ref, ws))[n]
        return pltpu.make_async_copy(src.at[l], dst.at[l], weight_sem.at[n, l])

    for r in range(rows):
        start_copy(r).start()
    for l in range(layers):
        for n in range(2):
            weight_copy(n, l).start()
    gain_copy = pltpu.make_async_copy(gain_ref, gains, gain_sem)
    gain_copy.start()

    barrier = pltpu.get_barrier_semaphore()
    meets = [
        (s > 0, (d, s - 1)),
        (s < spaces - 1, (d, s + 1)),
        (d > 0, (d - 1, s)),
        (d < depths - 1, (d + 1, s)),
        (d > 1, (d - 2, s)),
        (d < depths - 2, (d + 2, s)),
    ]

    def greet(there, device):
        @pl.when(there)
        def _():
            pl.semaphore_signal(barrier, inc=1, device_id=device, device_id_type=MESH)

    for there, device in meets:
        greet(there, device)
    pl.semaphore_wait(barrier, sum(there.astype(jnp.int32) for there, _ in meets))

    def pair_copy(i, r):
        return pltpu.make_async_remote_copy(
            src_ref=own.at[i, r],
            dst_ref=pair_in.at[i, r],
            send_sem=pair_send.at[i, r],
            recv_sem=pair_recv.at[i, r],
            device_id=(d, pair),
            device_id_type=MESH,
        )

    def edge_copy(i, r):
        return pltpu.make_async_remote_copy(
            src_ref=own.at[i, r],
            dst_ref=edge_in.at[i, r],
            send_sem=edge_send.at[i, r],
            recv_sem=edge_recv.at[i, r],
            device_id=(d, across),
            device_id_type=MESH,
        )

    def share(i, which):
        for r in which:
            pair_copy(i, r).start()

        @pl.when(inside)
        def _():
            for r in reversed(which):
                edge_copy(i, r).start()

    column = lax.broadcasted_iota(jnp.int32, (cols, chans), 0)

    def put(slot, row, v):
        left = jnp.where(column == 0, 0.0, pltpu.roll(v, 1, 0))
        right = jnp.where(column == cols - 1, 0.0, pltpu.roll(v, cols - 1, 0))
        X[slot, row, 0] = left.astype(BF16)
        X[slot, row, 1] = v.astype(BF16)
        X[slot, row, 2] = right.astype(BF16)

    none = jnp.zeros((chans, chans), BF16)

    for r in range(rows):
        start_copy(r).wait()
        own[0, r] = S[0, rows + r].astype(BF16)
    share(0, range(rows))
    for r in range(rows):
        put(0, rows + r, S[0, rows + r])
    for l in range(layers):
        for n in range(2):
            weight_copy(n, l).wait()
    gain_copy.wait()

    def y_copy(piece):
        part = pl.ds(piece * half, half)
        return pltpu.make_async_remote_copy(
            src_ref=ybuf.at[part],
            dst_ref=own.at[1, part],
            send_sem=y_send.at[piece],
            recv_sem=y_recv.at[piece],
            device_id=(d + 1, s),
            device_id_type=MESH,
        )

    part = cols // 2
    mine = odd * half
    theirs = half - mine

    def scan_copy(kind, r, h, src, dst, device):
        return pltpu.make_async_remote_copy(
            src_ref=src.at[r, pl.ds(h * part, part)],
            dst_ref=dst.at[r, pl.ds(h * part, part)],
            send_sem=scan_send.at[kind, r, h],
            recv_sem=scan_recv.at[kind, r, h],
            device_id=(device, s),
            device_id_type=MESH,
        )

    def out_copy(l, r):
        return pltpu.make_async_copy(
            S.at[l + 1, rows + r], states_ref.at[l, image_row(r)], out_sem.at[l, r]
        )

    def relaxed_copy(r):
        return pltpu.make_async_copy(
            S.at[layers, rows + r], relaxed_ref.at[0, image_row(r)], relaxed_sem.at[r]
        )

    def piece_done(i, piece):
        which = range(piece * half, (piece + 1) * half)

        @pl.when(i == 0)
        def _():
            for r in which:
                ybuf[r] = S[layers, rows + r].astype(BF16)

            @pl.when(d < depths - 1)
            def _():
                y_copy(piece).start()

        @pl.when(i == 1)
        def _():
            @pl.when(odd == 1 - piece)
            def _():
                for r in which:
                    k = r - piece * half
                    qsend[k] = (S[layers, rows + r] - ybuf[r].astype(F32)).astype(BF16)
                    for h in range(2):
                        scan_copy(0, k, h, qsend, qrecv, partner).start()

            for r in which:
                relaxed_copy(r).start()

        @pl.when(i == 2)
        def _():
            for r in which:
                out_copy(layers - 1, r).start()

    def next_start():
        for piece in range(2):
            which = range(piece * half, (piece + 1) * half)

            @pl.when(d > 0)
            def _():
                y_copy(piece).wait_recv()
                for r in which:
                    S[0, rows + r] = own[1, r].astype(F32)

            @pl.when(d == 0)
            def _():
                for r in which:
                    own[1, r] = own[0, r]

            share(1, which)
            for r in which:
                put(0, rows + r, S[0, rows + r])

    def correct():
        even = d - odd
        gain_odd = gains[pl.ds((even + 1) % depths, 1), :]
        gain_next = gains[pl.ds((even + 2) % depths, 1), :]

        def start_row(r):
            own[2, r] = S[1, rows + r].astype(BF16)
            pair_copy(2, r).start()

            @pl.when(inside)
            def _():
                edge_copy(2, r).start()

        @pl.when(d < 2)
        def _():
            trecv[...] = jnp.zeros_like(trecv)

        for r in range(half):
            for h in range(2):
                piece = pl.ds(h * part, part)
                own_q = S[layers, rows + mine + r, piece] - ybuf[mine + r, piece].astype(F32)
                scan_copy(0, r, h, qsend, qrecv, partner).wait_recv()
                other = qrecv[r, piece].astype(F32)
                q_even = jnp.where(odd == 0, own_q, other)
                q_odd = jnp.where(odd == 0, other, own_q)

                @pl.when(d > 1)
                def _():
                    scan_copy(1, r, h, tsend, trecv, d + 2).wait_recv()

                e_even = trecv[r, piece].astype(F32)
                e_odd = gain_odd * e_even + q_even

                @pl.when(d < depths - 2)
                def _():
                    tsend[r, piece] = (gain_next * e_odd + q_odd).astype(BF16)
                    scan_copy(1, r, h, tsend, trecv, d + 2).start()

                fsend[r, piece] = jnp.where(odd == 0, e_odd, e_even).astype(BF16)
                scan_copy(2, r, h, fsend, frecv, partner).start()
                S[1, rows + mine + r, piece] = S[0, rows + mine + r, piece] + jnp.where(
                    odd == 0, e_even, e_odd
                )
            start_row(mine + r)

        for r in range(half):
            for h in range(2):
                scan_copy(2, r, h, fsend, frecv, partner).wait_recv()
            S[1, rows + theirs + r] = S[0, rows + theirs + r] + frecv[r].astype(F32)
            start_row(theirs + r)

        for r in range(rows):
            relaxed_copy(r).wait()
            out_copy(0, r).start()
            put(2, rows + r, S[1, rows + r])

    def sweep(i, carry):
        late = i // 2

        def step(k, starts):
            weights, l = (wf, ws)[1 - k % 2], (k + 1) // 2
            index = l - 1 - late
            lhs = jnp.concatenate(
                [
                    jnp.concatenate(
                        [X[k - 1, r + j - 1, b] for j in range(4) for b in range(3)], axis=1
                    )
                    for r in starts
                ],
                axis=0,
            )
            weight = pair_weight(
                lambda a, b: weights[index, 3 * (a + flip * (2 - 2 * a)) + b], none
            )
            out = jnp.tanh(jnp.dot(lhs, weight, preferred_element_type=F32))
            for n, first in enumerate(starts):
                for j in range(2):
                    row = first + j
                    v = out[n * cols : (n + 1) * cols, j * chans : (j + 1) * chans]
                    if k % 2 == 0:
                        v = S[l - 1, row] + 0.5 * v
                        S[l, row] = v
                    if k < convs:
                        put(k, row, v if row < far else jnp.where(inside, v, 0.0))

        def near(k):
            todo = list(range(k, far - k, 2))
            for g in range(0, len(todo), 2):
                step(k, todo[g : g + 2])

        def wide(k, piece):
            step(k, [far - k + piece * half, far - k + piece * half + 2])

        for r in range(rows):
            pair_copy(i, r).wait_recv()
        for r in range(rows):
            v = pair_in[i, r].astype(F32)
            S[late, rows - 1 - r] = v
            put(2 * late, rows - 1 - r, v)

        @pl.when(i < 2)
        def _():
            for k in (1, 2):
                near(k)

        for k in range(3, convs):
            near(k)

        @pl.when(inside)
        def _():
            for r in range(rows):
                edge_copy(i, r).wait_recv()

        for r in range(rows):
            v = jnp.where(inside, edge_in[i, r].astype(F32), 0.0)
            S[late, far + rows - 1 - r] = v
            put(2 * late, far + rows - 1 - r, v)

        @pl.when(i < 2)
        def _():
            for k in (1, 2):
                for piece in range(2):
                    wide(k, piece)

        wide(3, 0)
        for k in range(4, convs + 1):
            wide(k, 0)
            if k < convs:
                wide(k - 1, 1)

        @pl.when(i == 2)
        def _():
            for l in range(1, layers - 1):
                for r in range(rows):
                    out_copy(l, r).start()

        piece_done(i, 0)
        wide(convs - 1, 1)
        wide(convs, 1)
        piece_done(i, 1)

        @pl.when(i == 0)
        def _():
            next_start()

        @pl.when(i == 1)
        def _():
            correct()

        return carry

    @pl.when(jnp.logical_not(inside))
    def _():
        edge_in[...] = jnp.zeros_like(edge_in)

    lax.fori_loop(0, 3, sweep, 0)

    @pl.when(d < depths - 1)
    def _():
        for piece in range(2):
            y_copy(piece).wait_send()

    for r in range(half):
        for h in range(2):
            scan_copy(0, r, h, qsend, qrecv, partner).wait_send()
            scan_copy(2, r, h, fsend, frecv, partner).wait_send()

            @pl.when(d < depths - 2)
            def _():
                scan_copy(1, r, h, tsend, trecv, d + 2).wait_send()

    for i in range(3):
        for r in range(rows):
            pair_copy(i, r).wait_send()

        @pl.when(inside)
        def _():
            for r in range(rows):
                edge_copy(i, r).wait_send()

    for l in range(layers):
        for r in range(rows):
            out_copy(l, r).wait()


def shards(depths, spaces, coarse_states, first_kernels, second_kernels, coarse_channel_gain):
    layers, taps, chans, _ = first_kernels.shape
    _, rows, cols, _ = coarse_states.shape
    assert rows == 2 * layers and spaces % 2 == 0 and depths % 2 == 0
    half = rows // 2
    hbm = pl.BlockSpec(memory_space=pl.ANY)
    part = pltpu.VMEM((half, cols, chans), BF16)
    slabs = pltpu.VMEM((3, rows, cols, chans), BF16)
    dma = pltpu.SemaphoreType.DMA
    return pl.pallas_call(
        functools.partial(cycle_kernel, depths, spaces),
        out_shape=(
            jax.ShapeDtypeStruct((layers, rows, cols, chans), F32),
            jax.ShapeDtypeStruct((1, rows, cols, chans), F32),
        ),
        in_specs=[hbm] * 4,
        out_specs=(hbm, hbm),
        scratch_shapes=[
            pltpu.VMEM((layers, taps, chans, chans), BF16),
            pltpu.VMEM((layers, taps, chans, chans), BF16),
            pltpu.VMEM(coarse_channel_gain.shape, F32),
            pltpu.VMEM((2 * layers, 3 * rows, 3, cols, chans), BF16),
            pltpu.VMEM((layers + 1, 3 * rows, cols, chans), F32),
            slabs,
            slabs,
            slabs,
            pltpu.VMEM((rows, cols, chans), BF16),
            part,
            part,
            part,
            part,
            part,
            part,
            dma((rows,)),
            dma((2, layers)),
            dma,
            dma((3, rows)),
            dma((3, rows)),
            dma((3, rows)),
            dma((3, rows)),
            dma((2,)),
            dma((2,)),
            dma((3, half, 2)),
            dma((3, half, 2)),
            dma((layers, rows)),
            dma((rows,)),
        ],
        compiler_params=pltpu.CompilerParams(
            collective_id=0, has_side_effects=True, vmem_limit_bytes=52 * 1024 * 1024
        ),
    )(coarse_states[0], first_kernels, second_kernels, coarse_channel_gain)


def solution(mesh):
    depths, spaces = mesh.shape["depth"], mesh.shape["space"]
    placed = (
        P("depth", "space", None, None),
        P("depth", None, None, None),
        P("depth", None, None, None),
        P(),
    )
    return jax.shard_map(
        functools.partial(shards, depths, spaces),
        mesh=mesh,
        in_specs=placed,
        out_specs=(P("depth", "space", None, None), P("depth", "space", None, None)),
        check_vma=False,
    )
```

```python
import functools

import jax
import jax.numpy as jnp
from jax import lax
from jax.experimental import pallas as pl
from jax.experimental.pallas import tpu as pltpu
from jax.sharding import PartitionSpec as P

MESH = pl.DeviceIdType.MESH
F32 = jnp.float32
BF16 = jnp.bfloat16


def pair_weight(tap, none):
    blocks = []
    for i in range(4):
        for b in range(3):
            one = tap(i, b) if i < 3 else none
            two = tap(i - 1, b) if i > 0 else none
            blocks.append(jnp.concatenate([one, two], axis=1))
    return jnp.concatenate(blocks, axis=0)


def cycle_kernel(
    depths,
    spaces,
    start_ref,
    first_ref,
    second_ref,
    gain_ref,
    states_ref,
    relaxed_ref,
    wf,
    ws,
    gains,
    X,
    S,
    own,
    pair_in,
    mid_in,
    edge_in,
    ybuf,
    qsend,
    qrecv,
    tsend,
    trecv,
    fsend,
    frecv,
    start_sem,
    weight_sem,
    gain_sem,
    pair_send,
    pair_recv,
    mid_send,
    mid_recv,
    edge_send,
    edge_recv,
    y_send,
    y_recv,
    scan_send,
    scan_recv,
    out_sem,
    relaxed_sem,
):
    layers = first_ref.shape[0]
    rows, cols, chans = start_ref.shape
    convs = 2 * layers
    far = 2 * rows
    half = rows // 2
    d = lax.axis_index("depth")
    s = lax.axis_index("space")
    odd = d % 2
    partner = d + 1 - 2 * odd
    flip = 1 - s % 2
    pair = s + 1 - 2 * (s % 2)
    across = s - 1 + 2 * (s % 2)
    inside = (across >= 0) & (across < spaces)

    def image_row(r):
        return r + flip * (rows - 1 - 2 * r)

    def start_copy(r):
        return pltpu.make_async_copy(
            start_ref.at[image_row(r)], S.at[0, rows + r], start_sem.at[r]
        )

    def weight_copy(n, l):
        src, dst = ((first_ref, wf), (second_ref, ws))[n]
        return pltpu.make_async_copy(src.at[l], dst.at[l], weight_sem.at[n, l])

    for r in range(rows):
        start_copy(r).start()
    for l in range(layers):
        for n in range(2):
            weight_copy(n, l).start()
    gain_copy = pltpu.make_async_copy(gain_ref, gains, gain_sem)
    gain_copy.start()

    barrier = pltpu.get_barrier_semaphore()
    meets = [
        (s > 0, (d, s - 1)),
        (s < spaces - 1, (d, s + 1)),
        (d > 0, (d - 1, s)),
        (d < depths - 1, (d + 1, s)),
        (d > 1, (d - 2, s)),
        (d < depths - 2, (d + 2, s)),
    ]

    def greet(there, device):
        @pl.when(there)
        def _():
            pl.semaphore_signal(barrier, inc=1, device_id=device, device_id_type=MESH)

    for there, device in meets:
        greet(there, device)
    pl.semaphore_wait(barrier, sum(there.astype(jnp.int32) for there, _ in meets))

    def pair_copy(i, r):
        return pltpu.make_async_remote_copy(
            src_ref=own.at[i, r],
            dst_ref=pair_in.at[i, r],
            send_sem=pair_send.at[i, r],
            recv_sem=pair_recv.at[i, r],
            device_id=(d, pair),
            device_id_type=MESH,
        )

    def edge_copy(i, r):
        return pltpu.make_async_remote_copy(
            src_ref=own.at[i, r],
            dst_ref=edge_in.at[i, r],
            send_sem=edge_send.at[i, r],
            recv_sem=edge_recv.at[i, r],
            device_id=(d, across),
            device_id_type=MESH,
        )

    def mid_copy(i, r):
        return pltpu.make_async_remote_copy(
            src_ref=X.at[layers, rows + r, 1],
            dst_ref=mid_in.at[i, r],
            send_sem=mid_send.at[i, r],
            recv_sem=mid_recv.at[i, r],
            device_id=(d, pair),
            device_id_type=MESH,
        )

    def share(i, which):
        for r in which:
            if r < layers:
                pair_copy(i, r).start()

        @pl.when(inside)
        def _():
            for r in reversed(which):
                edge_copy(i, r).start()

    column = lax.broadcasted_iota(jnp.int32, (cols, chans), 0)

    def put(slot, row, v):
        left = jnp.where(column == 0, 0.0, pltpu.roll(v, 1, 0))
        right = jnp.where(column == cols - 1, 0.0, pltpu.roll(v, cols - 1, 0))
        X[slot, row, 0] = left.astype(BF16)
        X[slot, row, 1] = v.astype(BF16)
        X[slot, row, 2] = right.astype(BF16)

    none = jnp.zeros((chans, chans), BF16)

    for r in range(rows):
        start_copy(r).wait()
        own[0, r] = S[0, rows + r].astype(BF16)
    share(0, range(rows))
    for r in range(rows):
        put(0, rows + r, S[0, rows + r])
    for l in range(layers):
        for n in range(2):
            weight_copy(n, l).wait()
    gain_copy.wait()

    def y_copy(piece):
        part = pl.ds(piece * half, half)
        return pltpu.make_async_remote_copy(
            src_ref=ybuf.at[part],
            dst_ref=own.at[1, part],
            send_sem=y_send.at[piece],
            recv_sem=y_recv.at[piece],
            device_id=(d + 1, s),
            device_id_type=MESH,
        )

    part = cols // 2
    mine = odd * half
    theirs = half - mine

    def scan_copy(kind, r, h, src, dst, device):
        return pltpu.make_async_remote_copy(
            src_ref=src.at[r, pl.ds(h * part, part)],
            dst_ref=dst.at[r, pl.ds(h * part, part)],
            send_sem=scan_send.at[kind, r, h],
            recv_sem=scan_recv.at[kind, r, h],
            device_id=(device, s),
            device_id_type=MESH,
        )

    def out_copy(l, r):
        return pltpu.make_async_copy(
            S.at[l + 1, rows + r], states_ref.at[l, image_row(r)], out_sem.at[l, r]
        )

    def relaxed_copy(r):
        return pltpu.make_async_copy(
            S.at[layers, rows + r], relaxed_ref.at[0, image_row(r)], relaxed_sem.at[r]
        )

    def piece_done(i, piece):
        which = range(piece * half, (piece + 1) * half)

        @pl.when(i == 0)
        def _():
            for r in which:
                ybuf[r] = S[layers, rows + r].astype(BF16)

            @pl.when(d < depths - 1)
            def _():
                y_copy(piece).start()

        @pl.when(i == 1)
        def _():
            @pl.when(odd == 1 - piece)
            def _():
                for r in which:
                    k = r - piece * half
                    qsend[k] = (S[layers, rows + r] - ybuf[r].astype(F32)).astype(BF16)
                    for h in range(2):
                        scan_copy(0, k, h, qsend, qrecv, partner).start()

            for r in which:
                relaxed_copy(r).start()

        @pl.when(i == 2)
        def _():
            for r in which:
                out_copy(layers - 1, r).start()

    def next_start():
        for piece in range(2):
            which = range(piece * half, (piece + 1) * half)

            @pl.when(d > 0)
            def _():
                y_copy(piece).wait_recv()
                for r in which:
                    S[0, rows + r] = own[1, r].astype(F32)

            @pl.when(d == 0)
            def _():
                for r in which:
                    own[1, r] = own[0, r]

            share(1, which)
            for r in which:
                put(0, rows + r, S[0, rows + r])

    def correct():
        even = d - odd
        gain_odd = gains[pl.ds((even + 1) % depths, 1), :]
        gain_next = gains[pl.ds((even + 2) % depths, 1), :]

        def start_row(r):
            own[2, r] = S[1, rows + r].astype(BF16)

            @pl.when(r < layers - 2)
            def _():
                pair_copy(2, r).start()

            @pl.when(inside & (r > 1))
            def _():
                edge_copy(2, r).start()

        @pl.when(d < 2)
        def _():
            trecv[...] = jnp.zeros_like(trecv)

        for r in range(half):
            for h in range(2):
                piece = pl.ds(h * part, part)
                own_q = S[layers, rows + mine + r, piece] - ybuf[mine + r, piece].astype(F32)
                scan_copy(0, r, h, qsend, qrecv, partner).wait_recv()
                other = qrecv[r, piece].astype(F32)
                q_even = jnp.where(odd == 0, own_q, other)
                q_odd = jnp.where(odd == 0, other, own_q)

                @pl.when(d > 1)
                def _():
                    scan_copy(1, r, h, tsend, trecv, d + 2).wait_recv()

                e_even = trecv[r, piece].astype(F32)
                e_odd = gain_odd * e_even + q_even

                @pl.when(d < depths - 2)
                def _():
                    tsend[r, piece] = (gain_next * e_odd + q_odd).astype(BF16)
                    scan_copy(1, r, h, tsend, trecv, d + 2).start()

                fsend[r, piece] = jnp.where(odd == 0, e_odd, e_even).astype(BF16)
                scan_copy(2, r, h, fsend, frecv, partner).start()
                S[1, rows + mine + r, piece] = S[0, rows + mine + r, piece] + jnp.where(
                    odd == 0, e_even, e_odd
                )
            start_row(mine + r)

        for r in range(half):
            for h in range(2):
                scan_copy(2, r, h, fsend, frecv, partner).wait_recv()
            S[1, rows + theirs + r] = S[0, rows + theirs + r] + frecv[r].astype(F32)
            start_row(theirs + r)

        for r in range(rows):
            relaxed_copy(r).wait()
            out_copy(0, r).start()
            put(2, rows + r, S[1, rows + r])

    def step(late, k, starts):
        weights, l = (wf, ws)[1 - k % 2], (k + 1) // 2
        index = l - 1 - late
        weight = pair_weight(
            lambda a, b: weights[index, 3 * (a + flip * (2 - 2 * a)) + b], none
        )
        for g in range(0, len(starts), 2):
            group = starts[g : g + 2]
            lhs = jnp.concatenate(
                [
                    jnp.concatenate(
                        [X[k - 1, r + j - 1, b] for j in range(4) for b in range(3)], axis=1
                    )
                    for r in group
                ],
                axis=0,
            )
            out = jnp.tanh(jnp.dot(lhs, weight, preferred_element_type=F32))
            for n, first in enumerate(group):
                for j in range(2):
                    row = first + j
                    v = out[n * cols : (n + 1) * cols, j * chans : (j + 1) * chans]
                    if k % 2 == 0:
                        v = S[l - 1, row] + 0.5 * v
                        S[l, row] = v
                    if k < convs:
                        put(k, row, v if row < far else jnp.where(inside, v, 0.0))

    def low(k):
        return rows - layers + k if k <= layers else k

    def near(late, k):
        step(late, k, range(low(k), far - k, 2))

    def wide(late, k):
        step(late, k, range(far - k, far + rows - k, 2))

    def entry(late):
        return layers - 2 * late, range(2 * late, rows)

    def pair_rows(i, late):
        count, _ = entry(late)
        for r in range(count):
            pair_copy(i, r).wait_recv()
        for r in range(count):
            v = pair_in[i, r].astype(F32)
            S[late, rows - 1 - r] = v
            put(2 * late, rows - 1 - r, v)

    def edge_rows(i, late):
        _, which = entry(late)

        @pl.when(inside)
        def _():
            for r in which:
                edge_copy(i, r).wait_recv()

        for r in which:
            v = jnp.where(inside, edge_in[i, r].astype(F32), 0.0)
            S[late, far + rows - 1 - r] = v
            put(2 * late, far + rows - 1 - r, v)

    def sweep(i, carry):
        late = i // 2

        @pl.when(i < 2)
        def _():
            pair_rows(i, 0)
            for k in (1, 2, 3):
                near(0, k)
            edge_rows(i, 0)
            for k in (1, 2, 3):
                wide(0, k)

        @pl.when(i == 2)
        def _():
            pair_rows(i, 1)
            near(1, 3)
            edge_rows(i, 1)
            wide(1, 3)

        step(late, layers, range(rows, rows + layers, 2))
        for r in range(layers):
            mid_copy(i, r).start()
        step(late, layers, range(rows + layers, far + rows - layers, 2))
        cut = low(layers + 1) + layers + 2
        step(late, layers + 1, range(cut, far + rows - layers - 1, 2))
        for r in range(layers):
            mid_copy(i, r).wait()
        for r in range(layers):
            v = mid_in[i, r].astype(F32)
            S[layers // 2, rows - 1 - r] = v
            put(layers, rows - 1 - r, v)
        step(late, layers + 1, range(low(layers + 1), cut, 2))
        for k in range(layers + 2, convs):
            step(late, k, range(low(k), far + rows - k, 2))

        @pl.when(i == 2)
        def _():
            for l in range(1, layers - 1):
                for r in range(rows):
                    out_copy(l, r).start()

        step(late, convs, range(rows, far, 2))
        for piece in range(2):
            piece_done(i, piece)

        @pl.when(i == 0)
        def _():
            next_start()

        @pl.when(i == 1)
        def _():
            correct()

        return carry

    @pl.when(jnp.logical_not(inside))
    def _():
        edge_in[...] = jnp.zeros_like(edge_in)

    lax.fori_loop(0, 3, sweep, 0)

    @pl.when(d < depths - 1)
    def _():
        for piece in range(2):
            y_copy(piece).wait_send()

    for r in range(half):
        for h in range(2):
            scan_copy(0, r, h, qsend, qrecv, partner).wait_send()
            scan_copy(2, r, h, fsend, frecv, partner).wait_send()

            @pl.when(d < depths - 2)
            def _():
                scan_copy(1, r, h, tsend, trecv, d + 2).wait_send()

    for i in range(3):
        count, which = entry(i // 2)
        for r in range(count):
            pair_copy(i, r).wait_send()

        @pl.when(inside)
        def _():
            for r in which:
                edge_copy(i, r).wait_send()

    for l in range(layers):
        for r in range(rows):
            out_copy(l, r).wait()


def write_kernel(states_ref, relaxed_ref, states_out, relaxed_out, held, in_sem, out_sem):
    layers = states_ref.shape[0]
    places = [(states_ref, states_out, l, l) for l in range(layers)]
    places.append((relaxed_ref, relaxed_out, 0, layers))
    reads, writes = [], []
    for src, dst, n, at in places:
        reads.append(pltpu.make_async_copy(src.at[n], held.at[at], in_sem.at[at]))
        writes.append(pltpu.make_async_copy(held.at[at], dst.at[n], out_sem.at[at]))
    for copy in reads:
        copy.start()
    for read, write in zip(reads, writes):
        read.wait()
        write.start()
    for copy in writes:
        copy.wait()


def shards(depths, spaces, coarse_states, first_kernels, second_kernels, coarse_channel_gain):
    layers, taps, chans, _ = first_kernels.shape
    _, rows, cols, _ = coarse_states.shape
    assert rows == 2 * layers and layers == 4 and spaces % 2 == 0 and depths % 2 == 0
    half = rows // 2
    hbm = pl.BlockSpec(memory_space=pltpu.HBM)
    part = pltpu.VMEM((half, cols, chans), BF16)
    slabs = pltpu.VMEM((3, rows, cols, chans), BF16)
    few = pltpu.VMEM((3, layers, cols, chans), BF16)
    dma = pltpu.SemaphoreType.DMA
    results = (
        jax.ShapeDtypeStruct((layers, rows, cols, chans), F32),
        jax.ShapeDtypeStruct((1, rows, cols, chans), F32),
    )
    states, relaxed = pl.pallas_call(
        functools.partial(cycle_kernel, depths, spaces),
        out_shape=results,
        in_specs=[hbm] * 4,
        out_specs=(hbm, hbm),
        scratch_shapes=[
            pltpu.VMEM((layers, taps, chans, chans), BF16),
            pltpu.VMEM((layers, taps, chans, chans), BF16),
            pltpu.VMEM(coarse_channel_gain.shape, F32),
            pltpu.VMEM((2 * layers, 3 * rows, 3, cols, chans), BF16),
            pltpu.VMEM((layers + 1, 3 * rows, cols, chans), F32),
            slabs,
            few,
            few,
            slabs,
            pltpu.VMEM((rows, cols, chans), BF16),
            part,
            part,
            part,
            part,
            part,
            part,
            dma((rows,)),
            dma((2, layers)),
            dma,
            dma((3, layers)),
            dma((3, layers)),
            dma((3, layers)),
            dma((3, layers)),
            dma((3, rows)),
            dma((3, rows)),
            dma((2,)),
            dma((2,)),
            dma((3, half, 2)),
            dma((3, half, 2)),
            dma((layers, rows)),
            dma((rows,)),
        ],
        compiler_params=pltpu.CompilerParams(
            collective_id=0, has_side_effects=True, vmem_limit_bytes=58 * 1024 * 1024
        ),
    )(coarse_states[0], first_kernels, second_kernels, coarse_channel_gain)
    return pl.pallas_call(
        write_kernel,
        out_shape=results,
        in_specs=[hbm] * 2,
        out_specs=(hbm, hbm),
        scratch_shapes=[
            pltpu.VMEM((layers + 1, rows, cols, chans), F32),
            dma((layers + 1,)),
            dma((layers + 1,)),
        ],
    )(states, relaxed)


def solution(mesh):
    depths, spaces = mesh.shape["depth"], mesh.shape["space"]
    placed = (
        P("depth", "space", None, None),
        P("depth", None, None, None),
        P("depth", None, None, None),
        P(),
    )
    return jax.shard_map(
        functools.partial(shards, depths, spaces),
        mesh=mesh,
        in_specs=placed,
        out_specs=(P("depth", "space", None, None), P("depth", "space", None, None)),
        check_vma=False,
    )
```

```python
import functools

import jax
import jax.numpy as jnp
from jax import lax
from jax.experimental import pallas as pl
from jax.experimental.pallas import tpu as pltpu
from jax.sharding import PartitionSpec as P

MESH = pl.DeviceIdType.MESH
F32 = jnp.float32
BF16 = jnp.bfloat16


def pair_weight(tap, none):
    blocks = []
    for i in range(4):
        for b in range(3):
            one = tap(i, b) if i < 3 else none
            two = tap(i - 1, b) if i > 0 else none
            blocks.append(jnp.concatenate([one, two], axis=1))
    return jnp.concatenate(blocks, axis=0)


def column_windows(cols):
    part, lap = cols // 2, 16
    return (
        ((0, part + lap), (part, part)),
        ((0, part), (part - lap, part + lap)),
    )


def cycle_kernel(
    depths,
    spaces,
    start_ref,
    first_ref,
    second_ref,
    gain_ref,
    states_ref,
    relaxed_ref,
    wf,
    ws,
    gains,
    X,
    S,
    own,
    pair_in,
    mid_in,
    edge_in,
    ybuf,
    qsend,
    qrecv,
    tsend,
    trecv,
    fsend,
    frecv,
    start_sem,
    weight_sem,
    gain_sem,
    pair_send,
    pair_recv,
    mid_send,
    mid_recv,
    edge_send,
    edge_recv,
    y_send,
    y_recv,
    scan_send,
    scan_recv,
    out_sem,
    relaxed_sem,
):
    layers = first_ref.shape[0]
    rows, cols, chans = start_ref.shape
    convs = 2 * layers
    far = 2 * rows
    half = rows // 2
    part = cols // 2
    windows = column_windows(cols)
    d = lax.axis_index("depth")
    s = lax.axis_index("space")
    odd = d % 2
    partner = d + 1 - 2 * odd
    flip = 1 - s % 2
    pair = s + 1 - 2 * (s % 2)
    across = s - 1 + 2 * (s % 2)
    inside = (across >= 0) & (across < spaces)

    def image_row(r):
        return r + flip * (rows - 1 - 2 * r)

    def start_copy(r):
        return pltpu.make_async_copy(
            start_ref.at[image_row(r)], S.at[0, rows + r], start_sem.at[r]
        )

    def weight_copy(n, l):
        src, dst = ((first_ref, wf), (second_ref, ws))[n]
        return pltpu.make_async_copy(src.at[l], dst.at[l], weight_sem.at[n, l])

    for r in range(rows):
        start_copy(r).start()
    for l in range(layers):
        for n in range(2):
            weight_copy(n, l).start()
    gain_copy = pltpu.make_async_copy(gain_ref, gains, gain_sem)
    gain_copy.start()

    barrier = pltpu.get_barrier_semaphore()
    meets = [
        (s > 0, (d, s - 1)),
        (s < spaces - 1, (d, s + 1)),
        (d > 0, (d - 1, s)),
        (d < depths - 1, (d + 1, s)),
        (d > 1, (d - 2, s)),
        (d < depths - 2, (d + 2, s)),
    ]

    def greet(there, device):
        @pl.when(there)
        def _():
            pl.semaphore_signal(barrier, inc=1, device_id=device, device_id_type=MESH)

    for there, device in meets:
        greet(there, device)
    pl.semaphore_wait(barrier, sum(there.astype(jnp.int32) for there, _ in meets))

    def remote(src, dst, sends, recvs, at, device):
        return pltpu.make_async_remote_copy(
            src_ref=src,
            dst_ref=dst,
            send_sem=sends.at[at],
            recv_sem=recvs.at[at],
            device_id=device,
            device_id_type=MESH,
        )

    def entry(late):
        return layers - 2 * late

    def pair_copy(i, late, h):
        at = (i, h, pl.ds(0, entry(late)), pl.ds(0, windows[late][h][1]))
        return remote(own.at[at], pair_in.at[at], pair_send, pair_recv, (i, h), (d, pair))

    def mid_copy(i, late, h):
        start, width = windows[late][h]
        return remote(
            X.at[layers, pl.ds(rows, layers), 1, pl.ds(start, width)],
            mid_in.at[i, h, :, pl.ds(0, width)],
            mid_send,
            mid_recv,
            (i, h),
            (d, pair),
        )

    def edge_copy(i, late, h, piece):
        first = 2 * late if piece == 0 else half
        at = (i, h, pl.ds(first, half * (piece + 1) - first), pl.ds(0, windows[late][h][1]))
        return remote(
            own.at[at], edge_in.at[at], edge_send, edge_recv, (i, h, piece), (d, across)
        )

    def share(i, late, h, piece):
        if piece == 0:
            pair_copy(i, late, h).start()

        @pl.when(inside)
        def _():
            edge_copy(i, late, h, piece).start()

    def y_copy(h, piece):
        at = (pl.ds(piece * half, half), pl.ds(0, windows[0][h][1]))
        return remote(
            ybuf.at[(h,) + at], own.at[(1, h) + at], y_send, y_recv, (h, piece), (d + 1, s)
        )

    def scan_copy(kind, r, h, src, dst, device):
        at = (r, pl.ds(h * part, part))
        return remote(src.at[at], dst.at[at], scan_send, scan_recv, (kind, r, h), (device, s))

    def out_copy(l, r):
        return pltpu.make_async_copy(
            S.at[l + 1, rows + r], states_ref.at[l, image_row(r)], out_sem.at[l, r]
        )

    def relaxed_copy(r):
        return pltpu.make_async_copy(
            S.at[layers, rows + r], relaxed_ref.at[0, image_row(r)], relaxed_sem.at[r]
        )

    def put(late, h, slot, row, v):
        start, width = windows[late][h]
        column = lax.broadcasted_iota(jnp.int32, (width, chans), 0)
        left = pltpu.roll(v, 1, 0)
        right = pltpu.roll(v, width - 1, 0)
        if h == 0:
            left = jnp.where(column == 0, 0.0, left)
            X[slot, row, 0, pl.ds(start, width)] = left.astype(BF16)
        else:
            right = jnp.where(column == width - 1, 0.0, right)
            held = X[slot, row, 0, pl.ds(start, 16)].astype(F32)
            edge = jnp.where(column[:16] == 0, held, left[:16])
            X[slot, row, 0, pl.ds(start, 16)] = edge.astype(BF16)
            X[slot, row, 0, pl.ds(start + 16, width - 16)] = left[16:].astype(BF16)
        X[slot, row, 1, pl.ds(start, width)] = v.astype(BF16)
        X[slot, row, 2, pl.ds(start, width)] = right.astype(BF16)

    none = jnp.zeros((chans, chans), BF16)
    mine = odd * half
    theirs = half - mine

    def step(late, h, k, starts):
        start, width = windows[late][h]
        cut = pl.ds(start, width)
        weights, l = (wf, ws)[1 - k % 2], (k + 1) // 2
        index = l - 1 - late
        weight = pair_weight(
            lambda a, b: weights[index, 3 * (a + flip * (2 - 2 * a)) + b], none
        )
        for g in range(0, len(starts), 2):
            group = starts[g : g + 2]
            lhs = jnp.concatenate(
                [
                    jnp.concatenate(
                        [X[k - 1, r + j - 1, b, cut] for j in range(4) for b in range(3)], axis=1
                    )
                    for r in group
                ],
                axis=0,
            )
            out = jnp.tanh(jnp.dot(lhs, weight, preferred_element_type=F32))
            for n, first in enumerate(group):
                for j in range(2):
                    row = first + j
                    v = out[n * width : (n + 1) * width, j * chans : (j + 1) * chans]
                    if k % 2 == 0:
                        v = S[l - 1, row, cut] + 0.5 * v
                        S[l, row, cut] = v
                    if k < convs:
                        put(late, h, k, row, v if row < far else jnp.where(inside, v, 0.0))

    def low(k):
        return rows - layers + k if k <= layers else k

    def own_rows(late, h):
        cut = pl.ds(*windows[late][h])
        for r in range(rows):
            put(late, h, 2 * late, rows + r, S[late, rows + r, cut])

    def near(i, late, h):
        start, width = windows[late][h]
        pair_copy(i, late, h).wait_recv()
        for r in range(entry(late)):
            v = pair_in[i, h, r, pl.ds(0, width)].astype(F32)
            S[late, rows - 1 - r, pl.ds(start, width)] = v
            put(late, h, 2 * late, rows - 1 - r, v)
        for k in range(1 + 2 * late, 4):
            step(late, h, k, range(low(k), far - k, 2))

    def rest(i, late, h):
        start, width = windows[late][h]
        cut = pl.ds(start, width)

        @pl.when(inside)
        def _():
            for piece in range(2):
                edge_copy(i, late, h, piece).wait_recv()

        for r in range(2 * late, rows):
            v = jnp.where(inside, edge_in[i, h, r, pl.ds(0, width)].astype(F32), 0.0)
            S[late, far + rows - 1 - r, cut] = v
            put(late, h, 2 * late, far + rows - 1 - r, v)
        for k in range(1 + 2 * late, 4):
            step(late, h, k, range(far - k, far + rows - k, 2))
        step(late, h, layers, range(rows, rows + layers, 2))
        mid_copy(i, late, h).start()
        step(late, h, layers, range(rows + layers, far + rows - layers, 2))
        split = low(layers + 1) + layers + 2
        for k in (layers + 1, layers + 2):
            step(late, h, k, range(split + k - layers - 1, far + rows - k, 2))
        mid_copy(i, late, h).wait()
        for r in range(layers):
            v = mid_in[i, h, r, pl.ds(0, width)].astype(F32)
            S[layers // 2, rows - 1 - r, cut] = v
            put(late, h, layers, rows - 1 - r, v)
        for k in (layers + 1, layers + 2):
            step(late, h, k, range(low(k), split + k - layers - 1, 2))
        for k in range(layers + 3, convs):
            step(late, h, k, range(low(k), far + rows - k, 2))
        step(late, h, convs, range(rows, far, 2))

    def sent(i, h):
        @pl.when(i == 0)
        def _():
            start, width = windows[0][h]
            for r in range(rows):
                ybuf[h, r, pl.ds(0, width)] = S[layers, rows + r, pl.ds(start, width)].astype(BF16)

            @pl.when(d < depths - 1)
            def _():
                for piece in range(2):
                    y_copy(h, piece).start()

        @pl.when(i == 1)
        def _():
            cut = pl.ds(h * part, part)
            for k in range(half):
                r = theirs + k
                q = S[layers, rows + r, cut] - ybuf[h, r, pl.ds(0, part)].astype(F32)
                qsend[k, cut] = q.astype(BF16)
                scan_copy(0, k, h, qsend, qrecv, partner).start()
            if h == 1:
                for r in range(rows):
                    relaxed_copy(r).start()

    def shifted(h):
        start, width = windows[0][h]
        for piece in range(2):
            which = range(piece * half, (piece + 1) * half)

            @pl.when(d > 0)
            def _():
                y_copy(h, piece).wait_recv()
                for r in which:
                    S[0, rows + r, pl.ds(start, width)] = own[1, h, r, pl.ds(0, width)].astype(F32)

            @pl.when(d == 0)
            def _():
                for r in which:
                    own[1, h, r, pl.ds(0, width)] = own[0, h, r, pl.ds(0, width)]

            share(1, 0, h, piece)

    def corrected(h, piece):
        start, width = windows[1][h]
        for r in range(piece * half, (piece + 1) * half):
            own[2, h, r, pl.ds(0, width)] = S[1, rows + r, pl.ds(start, width)].astype(BF16)
        share(2, 1, h, piece)

    def chain(h):
        even = d - odd
        gain_odd = gains[pl.ds((even + 1) % depths, 1), :]
        gain_next = gains[pl.ds((even + 2) % depths, 1), :]
        cut = pl.ds(h * part, part)
        for r in range(half):
            own_q = S[layers, rows + mine + r, cut] - ybuf[h, mine + r, pl.ds(0, part)].astype(F32)
            scan_copy(0, r, h, qsend, qrecv, partner).wait_recv()
            other = qrecv[r, cut].astype(F32)
            q_even = jnp.where(odd == 0, own_q, other)
            q_odd = jnp.where(odd == 0, other, own_q)

            @pl.when(d > 1)
            def _():
                scan_copy(1, r, h, tsend, trecv, d + 2).wait_recv()

            e_even = trecv[r, cut].astype(F32)
            e_odd = gain_odd * e_even + q_even

            @pl.when(d < depths - 2)
            def _():
                tsend[r, cut] = (gain_next * e_odd + q_odd).astype(BF16)
                scan_copy(1, r, h, tsend, trecv, d + 2).start()

            fsend[r, cut] = jnp.where(odd == 0, e_odd, e_even).astype(BF16)
            scan_copy(2, r, h, fsend, frecv, partner).start()
            S[1, rows + mine + r, cut] = S[0, rows + mine + r, cut] + jnp.where(
                odd == 0, e_even, e_odd
            )
        for piece in range(2):

            @pl.when(odd == piece)
            def _():
                corrected(h, piece)

    def finish(h):
        cut = pl.ds(h * part, part)
        for r in range(half):
            scan_copy(2, r, h, fsend, frecv, partner).wait_recv()
            S[1, rows + theirs + r, cut] = S[0, rows + theirs + r, cut] + frecv[r, cut].astype(F32)
        for piece in range(2):

            @pl.when(odd == 1 - piece)
            def _():
                corrected(h, piece)

    @pl.when(jnp.logical_not(inside))
    def _():
        edge_in[...] = jnp.zeros_like(edge_in)

    @pl.when(d < 2)
    def _():
        trecv[...] = jnp.zeros_like(trecv)

    for r in range(rows):
        start_copy(r).wait()
    for h in range(2):
        start, width = windows[0][h]
        for r in range(rows):
            own[0, h, r, pl.ds(0, width)] = S[0, rows + r, pl.ds(start, width)].astype(BF16)
        for piece in (1, 0):
            share(0, 0, h, piece)
    for l in range(layers):
        for n in range(2):
            weight_copy(n, l).wait()
    gain_copy.wait()

    def sweep(i, carry):
        for h in range(2):

            @pl.when(i == 1)
            def _():
                shifted(h)

            own_rows(0, h)
            near(i, 0, h)
        for h in range(2):
            rest(i, 0, h)
            sent(i, h)
        return carry

    lax.fori_loop(0, 2, sweep, 0)

    for h in range(2):
        chain(h)
    finish(0)
    own_rows(1, 0)
    near(2, 1, 0)
    finish(1)
    for r in range(rows):
        out_copy(0, r).start()
    own_rows(1, 1)
    for r in range(rows):
        relaxed_copy(r).wait()
    rest(2, 1, 0)
    near(2, 1, 1)
    rest(2, 1, 1)
    for l in range(1, layers):
        for r in range(rows):
            out_copy(l, r).start()

    for h in range(2):

        @pl.when(d < depths - 1)
        def _():
            for piece in range(2):
                y_copy(h, piece).wait_send()

        for r in range(half):
            scan_copy(0, r, h, qsend, qrecv, partner).wait_send()
            scan_copy(2, r, h, fsend, frecv, partner).wait_send()

            @pl.when(d < depths - 2)
            def _():
                scan_copy(1, r, h, tsend, trecv, d + 2).wait_send()

        for i in range(3):
            pair_copy(i, i // 2, h).wait_send()

            @pl.when(inside)
            def _():
                for piece in range(2):
                    edge_copy(i, i // 2, h, piece).wait_send()

    for l in range(layers):
        for r in range(rows):
            out_copy(l, r).wait()


def write_kernel(states_ref, relaxed_ref, states_out, relaxed_out, held, in_sem, out_sem):
    layers = states_ref.shape[0]
    places = [(states_ref, states_out, l, l) for l in range(layers)]
    places.append((relaxed_ref, relaxed_out, 0, layers))
    reads, writes = [], []
    for src, dst, n, at in places:
        reads.append(pltpu.make_async_copy(src.at[n], held.at[at], in_sem.at[at]))
        writes.append(pltpu.make_async_copy(held.at[at], dst.at[n], out_sem.at[at]))
    for copy in reads:
        copy.start()
    for read, write in zip(reads, writes):
        read.wait()
        write.start()
    for copy in writes:
        copy.wait()


def shards(depths, spaces, coarse_states, first_kernels, second_kernels, coarse_channel_gain):
    layers, taps, chans, _ = first_kernels.shape
    _, rows, cols, _ = coarse_states.shape
    assert rows == 2 * layers and layers == 4 and spaces % 2 == 0 and depths % 2 == 0
    half = rows // 2
    wide = max(width for halves in column_windows(cols) for _, width in halves)
    hbm = pl.BlockSpec(memory_space=pltpu.HBM)
    part = pltpu.VMEM((half, cols, chans), BF16)
    slabs = pltpu.VMEM((3, 2, rows, wide, chans), BF16)
    few = pltpu.VMEM((3, 2, layers, wide, chans), BF16)
    dma = pltpu.SemaphoreType.DMA
    results = (
        jax.ShapeDtypeStruct((layers, rows, cols, chans), F32),
        jax.ShapeDtypeStruct((1, rows, cols, chans), F32),
    )
    states, relaxed = pl.pallas_call(
        functools.partial(cycle_kernel, depths, spaces),
        out_shape=results,
        in_specs=[hbm] * 4,
        out_specs=(hbm, hbm),
        scratch_shapes=[
            pltpu.VMEM((layers, taps, chans, chans), BF16),
            pltpu.VMEM((layers, taps, chans, chans), BF16),
            pltpu.VMEM(coarse_channel_gain.shape, F32),
            pltpu.VMEM((2 * layers, 3 * rows, 3, cols, chans), BF16),
            pltpu.VMEM((layers + 1, 3 * rows, cols, chans), F32),
            slabs,
            few,
            few,
            slabs,
            pltpu.VMEM((2, rows, wide, chans), BF16),
            part,
            part,
            part,
            part,
            part,
            part,
            dma((rows,)),
            dma((2, layers)),
            dma,
            dma((3, 2)),
            dma((3, 2)),
            dma((3, 2)),
            dma((3, 2)),
            dma((3, 2, 2)),
            dma((3, 2, 2)),
            dma((2, 2)),
            dma((2, 2)),
            dma((3, half, 2)),
            dma((3, half, 2)),
            dma((layers, rows)),
            dma((rows,)),
        ],
        compiler_params=pltpu.CompilerParams(
            collective_id=0, has_side_effects=True, vmem_limit_bytes=58 * 1024 * 1024
        ),
    )(coarse_states[0], first_kernels, second_kernels, coarse_channel_gain)
    return pl.pallas_call(
        write_kernel,
        out_shape=results,
        in_specs=[hbm] * 2,
        out_specs=(hbm, hbm),
        scratch_shapes=[
            pltpu.VMEM((layers + 1, rows, cols, chans), F32),
            dma((layers + 1,)),
            dma((layers + 1,)),
        ],
    )(states, relaxed)


def solution(mesh):
    depths, spaces = mesh.shape["depth"], mesh.shape["space"]
    placed = (
        P("depth", "space", None, None),
        P("depth", None, None, None),
        P("depth", None, None, None),
        P(),
    )
    return jax.shard_map(
        functools.partial(shards, depths, spaces),
        mesh=mesh,
        in_specs=placed,
        out_specs=(P("depth", "space", None, None), P("depth", "space", None, None)),
        check_vma=False,
    )
```

```python
import functools

import jax
import jax.numpy as jnp
from jax import lax
from jax.experimental import pallas as pl
from jax.experimental.pallas import tpu as pltpu
from jax.sharding import PartitionSpec as P

MESH = pl.DeviceIdType.MESH
F32 = jnp.float32
BF16 = jnp.bfloat16


def pair_weight(tap, none):
    blocks = []
    for i in range(4):
        for b in range(3):
            one = tap(i, b) if i < 3 else none
            two = tap(i - 1, b) if i > 0 else none
            blocks.append(jnp.concatenate([one, two], axis=1))
    return jnp.concatenate(blocks, axis=0)


def column_windows(cols):
    part, lap = cols // 2, 16
    return (
        ((0, part + lap), (part, part)),
        ((0, part), (part - lap, part + lap)),
    )


def cycle_kernel(
    depths,
    spaces,
    start_ref,
    first_ref,
    second_ref,
    gain_ref,
    states_ref,
    relaxed_ref,
    wf,
    ws,
    gains,
    X,
    S,
    own,
    pair_in,
    mid_in,
    mid_out,
    edge_in,
    ybuf,
    qsend,
    qrecv,
    tsend,
    trecv,
    start_sem,
    weight_sem,
    gain_sem,
    pair_send,
    pair_recv,
    mid_send,
    mid_recv,
    edge_send,
    edge_recv,
    y_send,
    y_recv,
    scan_send,
    scan_recv,
    out_sem,
    relaxed_sem,
):
    layers = first_ref.shape[0]
    rows, cols, chans = start_ref.shape
    convs = 2 * layers
    far = 2 * rows
    half = rows // 2
    part = cols // 2
    windows = column_windows(cols)
    d = lax.axis_index("depth")
    s = lax.axis_index("space")
    odd = d % 2
    partner = d + 1 - 2 * odd
    flip = 1 - s % 2
    pair = s + 1 - 2 * (s % 2)
    across = s - 1 + 2 * (s % 2)
    inside = (across >= 0) & (across < spaces)

    def image_row(r):
        return r + flip * (rows - 1 - 2 * r)

    def start_copy(r):
        return pltpu.make_async_copy(
            start_ref.at[image_row(r)], S.at[0, rows + r], start_sem.at[r]
        )

    def weight_copy(n, l):
        src, dst = ((first_ref, wf), (second_ref, ws))[n]
        return pltpu.make_async_copy(src.at[l], dst.at[l], weight_sem.at[n, l])

    for r in range(rows):
        start_copy(r).start()
    for l in range(layers):
        for n in range(2):
            weight_copy(n, l).start()
    gain_copy = pltpu.make_async_copy(gain_ref, gains, gain_sem)
    gain_copy.start()

    barrier = pltpu.get_barrier_semaphore()
    meets = [
        (s > 0, (d, s - 1)),
        (s < spaces - 1, (d, s + 1)),
        (d > 0, (d - 1, s)),
        (d < depths - 1, (d + 1, s)),
        (d > 1, (d - 2, s)),
        (d < depths - 2, (d + 2, s)),
    ]

    def greet(there, device):
        @pl.when(there)
        def _():
            pl.semaphore_signal(barrier, inc=1, device_id=device, device_id_type=MESH)

    for there, device in meets:
        greet(there, device)
    pl.semaphore_wait(barrier, sum(there.astype(jnp.int32) for there, _ in meets))

    def remote(src, dst, sends, recvs, at, device):
        return pltpu.make_async_remote_copy(
            src_ref=src,
            dst_ref=dst,
            send_sem=sends.at[at],
            recv_sem=recvs.at[at],
            device_id=device,
            device_id_type=MESH,
        )

    def entry(late):
        return layers - 2 * late

    def pair_copy(i, late, h):
        at = (i, h, pl.ds(0, entry(late)), pl.ds(0, windows[late][h][1]))
        return remote(own.at[at], pair_in.at[at], pair_send, pair_recv, (i, h), (d, pair))

    def mid_copy(i, late, h):
        cut = pl.ds(0, windows[late][h][1])
        return remote(
            mid_out.at[h, :, cut],
            mid_in.at[i, h, :, cut],
            mid_send,
            mid_recv,
            (i, h),
            (d, pair),
        )

    def edge_copy(i, late, h, piece):
        first = 2 * late if piece == 0 else half
        at = (i, h, pl.ds(first, half * (piece + 1) - first), pl.ds(0, windows[late][h][1]))
        return remote(
            own.at[at], edge_in.at[at], edge_send, edge_recv, (i, h, piece), (d, across)
        )

    def share(i, late, h, piece):
        if piece == 0:
            pair_copy(i, late, h).start()

        @pl.when(inside)
        def _():
            edge_copy(i, late, h, piece).start()

    def y_copy(h, piece):
        at = (pl.ds(piece * half, half), pl.ds(0, windows[0][h][1]))
        return remote(
            ybuf.at[(h,) + at], own.at[(1, h) + at], y_send, y_recv, (h, piece), (d + 1, s)
        )

    def scan_copy(kind, r, h, src, dst, device):
        at = (r, pl.ds(h * part, part))
        return remote(src.at[at], dst.at[at], scan_send, scan_recv, (kind, r, h), (device, s))

    def out_copy(l, r):
        return pltpu.make_async_copy(
            S.at[l + 1, rows + r], states_ref.at[l, image_row(r)], out_sem.at[l, r]
        )

    def relaxed_copy(r):
        return pltpu.make_async_copy(
            S.at[layers, rows + r], relaxed_ref.at[0, image_row(r)], relaxed_sem.at[r]
        )

    def put(late, h, slot, row, v):
        start, width = windows[late][h]
        column = lax.broadcasted_iota(jnp.int32, (width, chans), 0)
        left = pltpu.roll(v, 1, 0)
        right = pltpu.roll(v, width - 1, 0)
        if h == 0:
            left = jnp.where(column == 0, 0.0, left)
            X[slot, row, 0, pl.ds(start, width)] = left.astype(BF16)
        else:
            right = jnp.where(column == width - 1, 0.0, right)
            held = X[slot, row, 0, pl.ds(start, 16)].astype(F32)
            edge = jnp.where(column[:16] == 0, held, left[:16])
            X[slot, row, 0, pl.ds(start, 16)] = edge.astype(BF16)
            X[slot, row, 0, pl.ds(start + 16, width - 16)] = left[16:].astype(BF16)
        X[slot, row, 1, pl.ds(start, width)] = v.astype(BF16)
        X[slot, row, 2, pl.ds(start, width)] = right.astype(BF16)

    none = jnp.zeros((chans, chans), BF16)

    def step(late, h, k, starts):
        start, width = windows[late][h]
        cut = pl.ds(start, width)
        weights, l = (wf, ws)[1 - k % 2], (k + 1) // 2
        index = l - 1 - late
        weight = pair_weight(
            lambda a, b: weights[index, 3 * (a + flip * (2 - 2 * a)) + b], none
        )
        for g in range(0, len(starts), 2):
            group = starts[g : g + 2]
            lhs = jnp.concatenate(
                [
                    jnp.concatenate(
                        [X[k - 1, r + j - 1, b, cut] for j in range(4) for b in range(3)], axis=1
                    )
                    for r in group
                ],
                axis=0,
            )
            out = jnp.tanh(jnp.dot(lhs, weight, preferred_element_type=F32))
            for n, first in enumerate(group):
                for j in range(2):
                    row = first + j
                    v = out[n * width : (n + 1) * width, j * chans : (j + 1) * chans]
                    if k % 2 == 0:
                        v = S[l - 1, row, cut] + 0.5 * v
                        S[l, row, cut] = v
                    if k < convs:
                        put(late, h, k, row, v if row < far else jnp.where(inside, v, 0.0))

    def low(k):
        return rows - layers + k if k <= layers else k

    def own_rows(late, h):
        cut = pl.ds(*windows[late][h])
        for r in range(rows):
            put(late, h, 2 * late, rows + r, S[late, rows + r, cut])

    def near_own(late, h):
        own_rows(late, h)
        for k in range(1 + 2 * late, layers):
            step(late, h, k, range(rows + k - 2 * late, far - k, 2))

    def near_pair(i, late, h):
        start, width = windows[late][h]
        pair_copy(i, late, h).wait_recv()
        for r in range(entry(late)):
            v = pair_in[i, h, r, pl.ds(0, width)].astype(F32)
            S[late, rows - 1 - r, pl.ds(start, width)] = v
            put(late, h, 2 * late, rows - 1 - r, v)
        for k in range(1 + 2 * late, layers):
            step(late, h, k, range(low(k), rows + k - 2 * late, 2))
        step(late, h, layers, range(rows, rows + layers, 2))
        for r in range(layers):
            mid_out[h, r, pl.ds(0, width)] = X[layers, rows + r, 1, pl.ds(start, width)]
        mid_copy(i, late, h).start()

    def state_out(late, h, k):
        if late and h == 1 and k % 2 == 0:
            for r in range(rows):
                out_copy(k // 2 - 1, r).start()

    def rest(i, late, h):
        start, width = windows[late][h]
        cut = pl.ds(start, width)

        @pl.when(inside)
        def _():
            for piece in range(2):
                edge_copy(i, late, h, piece).wait_recv()

        for r in range(2 * late, rows):
            v = jnp.where(inside, edge_in[i, h, r, pl.ds(0, width)].astype(F32), 0.0)
            S[late, far + rows - 1 - r, cut] = v
            put(late, h, 2 * late, far + rows - 1 - r, v)
        for k in range(1 + 2 * late, layers + 1):
            step(late, h, k, range(far - k, far + rows - k, 2))
        state_out(late, h, layers)
        split = low(layers + 1) + layers + 2
        step(late, h, layers + 1, range(split, far + rows - layers - 1, 2))
        mid_copy(i, late, h).wait()
        for r in range(layers):
            v = mid_in[i, h, r, pl.ds(0, width)].astype(F32)
            S[layers // 2, rows - 1 - r, cut] = v
            put(late, h, layers, rows - 1 - r, v)
        step(late, h, layers + 1, range(low(layers + 1), split, 2))
        for k in range(layers + 2, convs):
            step(late, h, k, range(low(k), far + rows - k, 2))
            state_out(late, h, k)
        step(late, h, convs, range(rows, far, 2))
        state_out(late, h, convs)

    def sent(i, h):
        @pl.when(i == 0)
        def _():
            start, width = windows[0][h]
            for r in range(rows):
                ybuf[h, r, pl.ds(0, width)] = S[layers, rows + r, pl.ds(start, width)].astype(BF16)

            @pl.when(d < depths - 1)
            def _():
                for piece in range(2):
                    y_copy(h, piece).start()

        @pl.when(i == 1)
        def _():
            cut = pl.ds(h * part, part)
            for r in range(rows):
                q = S[layers, rows + r, cut] - ybuf[h, r, pl.ds(0, part)].astype(F32)
                qsend[r, cut] = q.astype(BF16)
                scan_copy(0, r, h, qsend, qrecv, partner).start()
            if h == 1:
                for r in range(rows):
                    relaxed_copy(r).start()

    def shifted(h):
        start, width = windows[0][h]
        for piece in range(2):
            which = range(piece * half, (piece + 1) * half)

            @pl.when(d > 0)
            def _():
                y_copy(h, piece).wait_recv()
                for r in which:
                    S[0, rows + r, pl.ds(start, width)] = own[1, h, r, pl.ds(0, width)].astype(F32)

            @pl.when(d == 0)
            def _():
                for r in which:
                    own[1, h, r, pl.ds(0, width)] = own[0, h, r, pl.ds(0, width)]

            share(1, 0, h, piece)

    def corrected(h, piece):
        start, width = windows[1][h]
        for r in range(piece * half, (piece + 1) * half):
            own[2, h, r, pl.ds(0, width)] = S[1, rows + r, pl.ds(start, width)].astype(BF16)
        share(2, 1, h, piece)

    def chain(h):
        even = d - odd
        gain_odd = gains[pl.ds((even + 1) % depths, 1), :]
        gain_next = gains[pl.ds((even + 2) % depths, 1), :]
        cut = pl.ds(h * part, part)
        for r in range(rows):
            own_q = S[layers, rows + r, cut] - ybuf[h, r, pl.ds(0, part)].astype(F32)
            scan_copy(0, r, h, qsend, qrecv, partner).wait_recv()
            other = qrecv[r, cut].astype(F32)
            q_even = jnp.where(odd == 0, own_q, other)
            q_odd = jnp.where(odd == 0, other, own_q)

            @pl.when(d > 1)
            def _():
                scan_copy(1, r, h, tsend, trecv, d + 2).wait_recv()

            e_even = trecv[r, cut].astype(F32)
            e_odd = gain_odd * e_even + q_even

            @pl.when(d < depths - 2)
            def _():
                tsend[r, cut] = (gain_next * e_odd + q_odd).astype(BF16)
                scan_copy(1, r, h, tsend, trecv, d + 2).start()

            S[1, rows + r, cut] = S[0, rows + r, cut] + jnp.where(odd == 0, e_even, e_odd)
            if r % half == half - 1:
                corrected(h, r // half)

    @pl.when(jnp.logical_not(inside))
    def _():
        edge_in[...] = jnp.zeros_like(edge_in)

    @pl.when(d < 2)
    def _():
        trecv[...] = jnp.zeros_like(trecv)

    for r in range(rows):
        start_copy(r).wait()
    for h in range(2):
        start, width = windows[0][h]
        for r in range(rows):
            own[0, h, r, pl.ds(0, width)] = S[0, rows + r, pl.ds(start, width)].astype(BF16)
        for piece in (1, 0):
            share(0, 0, h, piece)
    for l in range(layers):
        for n in range(2):
            weight_copy(n, l).wait()
    gain_copy.wait()

    def sweep(i, carry):
        for h in range(2):

            @pl.when(i == 1)
            def _():
                shifted(h)

            near_own(0, h)
            near_pair(i, 0, h)
        for h in range(2):
            rest(i, 0, h)
            sent(i, h)
        return carry

    lax.fori_loop(0, 2, sweep, 0)

    chain(0)
    chain(1)
    for r in range(rows):
        out_copy(0, r).start()
        relaxed_copy(r).wait()
    for h in range(2):
        near_own(1, h)
        near_pair(2, 1, h)
    for h in range(2):
        rest(2, 1, h)

    for h in range(2):

        @pl.when(d < depths - 1)
        def _():
            for piece in range(2):
                y_copy(h, piece).wait_send()

        for r in range(rows):
            scan_copy(0, r, h, qsend, qrecv, partner).wait_send()

            @pl.when(d < depths - 2)
            def _():
                scan_copy(1, r, h, tsend, trecv, d + 2).wait_send()

        for i in range(3):
            pair_copy(i, i // 2, h).wait_send()

            @pl.when(inside)
            def _():
                for piece in range(2):
                    edge_copy(i, i // 2, h, piece).wait_send()

    for l in range(layers):
        for r in range(rows):
            out_copy(l, r).wait()


def write_kernel(states_ref, relaxed_ref, states_out, relaxed_out, held, in_sem, out_sem):
    layers = states_ref.shape[0]
    places = [(states_ref, states_out, l, l) for l in range(layers)]
    places.append((relaxed_ref, relaxed_out, 0, layers))
    reads, writes = [], []
    for src, dst, n, at in places:
        reads.append(pltpu.make_async_copy(src.at[n], held.at[at], in_sem.at[at]))
        writes.append(pltpu.make_async_copy(held.at[at], dst.at[n], out_sem.at[at]))
    for copy in reads:
        copy.start()
    for read, write in zip(reads, writes):
        read.wait()
        write.start()
    for copy in writes:
        copy.wait()


def shards(depths, spaces, coarse_states, first_kernels, second_kernels, coarse_channel_gain):
    layers, taps, chans, _ = first_kernels.shape
    _, rows, cols, _ = coarse_states.shape
    assert rows == 2 * layers and layers == 4 and spaces % 2 == 0 and depths % 2 == 0
    wide = max(width for halves in column_windows(cols) for _, width in halves)
    hbm = pl.BlockSpec(memory_space=pltpu.HBM)
    field = pltpu.VMEM((rows, cols, chans), BF16)
    slabs = pltpu.VMEM((3, 2, rows, wide, chans), BF16)
    few = pltpu.VMEM((3, 2, layers, wide, chans), BF16)
    dma = pltpu.SemaphoreType.DMA
    results = (
        jax.ShapeDtypeStruct((layers, rows, cols, chans), F32),
        jax.ShapeDtypeStruct((1, rows, cols, chans), F32),
    )
    states, relaxed = pl.pallas_call(
        functools.partial(cycle_kernel, depths, spaces),
        out_shape=results,
        in_specs=[hbm] * 4,
        out_specs=(hbm, hbm),
        scratch_shapes=[
            pltpu.VMEM((layers, taps, chans, chans), BF16),
            pltpu.VMEM((layers, taps, chans, chans), BF16),
            pltpu.VMEM(coarse_channel_gain.shape, F32),
            pltpu.VMEM((2 * layers, 3 * rows, 3, cols, chans), BF16),
            pltpu.VMEM((layers + 1, 3 * rows, cols, chans), F32),
            slabs,
            few,
            few,
            pltpu.VMEM((2, layers, wide, chans), BF16),
            slabs,
            pltpu.VMEM((2, rows, wide, chans), BF16),
            field,
            field,
            field,
            field,
            dma((rows,)),
            dma((2, layers)),
            dma,
            dma((3, 2)),
            dma((3, 2)),
            dma((3, 2)),
            dma((3, 2)),
            dma((3, 2, 2)),
            dma((3, 2, 2)),
            dma((2, 2)),
            dma((2, 2)),
            dma((2, rows, 2)),
            dma((2, rows, 2)),
            dma((layers, rows)),
            dma((rows,)),
        ],
        compiler_params=pltpu.CompilerParams(
            collective_id=0, has_side_effects=True, vmem_limit_bytes=58 * 1024 * 1024
        ),
    )(coarse_states[0], first_kernels, second_kernels, coarse_channel_gain)
    return pl.pallas_call(
        write_kernel,
        out_shape=results,
        in_specs=[hbm] * 2,
        out_specs=(hbm, hbm),
        scratch_shapes=[
            pltpu.VMEM((layers + 1, rows, cols, chans), F32),
            dma((layers + 1,)),
            dma((layers + 1,)),
        ],
    )(states, relaxed)


def solution(mesh):
    depths, spaces = mesh.shape["depth"], mesh.shape["space"]
    placed = (
        P("depth", "space", None, None),
        P("depth", None, None, None),
        P("depth", None, None, None),
        P(),
    )
    return jax.shard_map(
        functools.partial(shards, depths, spaces),
        mesh=mesh,
        in_specs=placed,
        out_specs=(P("depth", "space", None, None), P("depth", "space", None, None)),
        check_vma=False,
    )
```

```python
import functools

import jax
import jax.numpy as jnp
from jax import lax
from jax.experimental import pallas as pl
from jax.experimental.pallas import tpu as pltpu
from jax.sharding import PartitionSpec as P

MESH = pl.DeviceIdType.MESH
F32 = jnp.float32
BF16 = jnp.bfloat16


def pair_weight(tap, none):
    blocks = []
    for i in range(4):
        for b in range(3):
            one = tap(i, b) if i < 3 else none
            two = tap(i - 1, b) if i > 0 else none
            blocks.append(jnp.concatenate([one, two], axis=1))
    return jnp.concatenate(blocks, axis=0)


def column_windows(cols):
    part, lap = cols // 2, 16
    return (0, part + lap), (part, part), (0, cols)


WHOLE = 2


def cycle_kernel(
    depths,
    spaces,
    start_ref,
    first_ref,
    second_ref,
    gain_ref,
    states_ref,
    relaxed_ref,
    wf,
    ws,
    gains,
    X,
    S,
    own,
    pair_in,
    mid_in,
    mid_out,
    edge_in,
    ybuf,
    qsend,
    qrecv,
    tsend,
    trecv,
    start_sem,
    weight_sem,
    gain_sem,
    pair_send,
    pair_recv,
    mid_send,
    mid_recv,
    edge_send,
    edge_recv,
    y_send,
    y_recv,
    scan_send,
    scan_recv,
    out_sem,
    relaxed_sem,
):
    layers = first_ref.shape[0]
    rows, cols, chans = start_ref.shape
    convs = 2 * layers
    far = 2 * rows
    half = rows // 2
    part = cols // 2
    windows = column_windows(cols)
    d = lax.axis_index("depth")
    s = lax.axis_index("space")
    odd = d % 2
    partner = d + 1 - 2 * odd
    flip = 1 - s % 2
    pair = s + 1 - 2 * (s % 2)
    across = s - 1 + 2 * (s % 2)
    inside = (across >= 0) & (across < spaces)

    def image_row(r):
        return r + flip * (rows - 1 - 2 * r)

    def start_copy(r):
        return pltpu.make_async_copy(
            start_ref.at[image_row(r)], S.at[0, rows + r], start_sem.at[r]
        )

    def weight_copy(n, l):
        src, dst = ((first_ref, wf), (second_ref, ws))[n]
        return pltpu.make_async_copy(src.at[l], dst.at[l], weight_sem.at[n, l])

    for r in range(rows):
        start_copy(r).start()
    for l in range(layers):
        for n in range(2):
            weight_copy(n, l).start()
    gain_copy = pltpu.make_async_copy(gain_ref, gains, gain_sem)
    gain_copy.start()

    barrier = pltpu.get_barrier_semaphore()
    meets = [
        (s > 0, (d, s - 1)),
        (s < spaces - 1, (d, s + 1)),
        (d > 0, (d - 1, s)),
        (d < depths - 1, (d + 1, s)),
        (d > 1, (d - 2, s)),
        (d < depths - 2, (d + 2, s)),
    ]

    def greet(there, device):
        @pl.when(there)
        def _():
            pl.semaphore_signal(barrier, inc=1, device_id=device, device_id_type=MESH)

    for there, device in meets:
        greet(there, device)
    pl.semaphore_wait(barrier, sum(there.astype(jnp.int32) for there, _ in meets))

    def remote(src, dst, sends, recvs, at, device):
        return pltpu.make_async_remote_copy(
            src_ref=src,
            dst_ref=dst,
            send_sem=sends.at[at],
            recv_sem=recvs.at[at],
            device_id=device,
            device_id_type=MESH,
        )

    def entry(late):
        return layers - 2 * late

    def sent_width(late, h):
        return part if late else windows[h][1]

    def pair_copy(i, late, h):
        at = (i, h, pl.ds(0, entry(late)), pl.ds(0, sent_width(late, h)))
        return remote(own.at[at], pair_in.at[at], pair_send, pair_recv, (i, h), (d, pair))

    def mid_copy(i, h):
        n, cut = h % 2, pl.ds(0, windows[h][1])
        return remote(
            mid_out.at[n, :, cut],
            mid_in.at[i, n, :, cut],
            mid_send,
            mid_recv,
            (i, n),
            (d, pair),
        )

    def edge_copy(i, late, h, piece):
        first = 2 * late if piece == 0 else half
        at = (i, h, pl.ds(first, half * (piece + 1) - first), pl.ds(0, sent_width(late, h)))
        return remote(
            own.at[at], edge_in.at[at], edge_send, edge_recv, (i, h, piece), (d, across)
        )

    def share(i, late, h, piece):
        if piece == 0:
            pair_copy(i, late, h).start()

        @pl.when(inside)
        def _():
            edge_copy(i, late, h, piece).start()

    def y_copy(h, piece):
        at = (pl.ds(piece * half, half), pl.ds(0, windows[h][1]))
        return remote(
            ybuf.at[(h,) + at], own.at[(1, h) + at], y_send, y_recv, (h, piece), (d + 1, s)
        )

    def scan_copy(kind, r, h, src, dst, device):
        at = (r, pl.ds(h * part, part))
        return remote(src.at[at], dst.at[at], scan_send, scan_recv, (kind, r, h), (device, s))

    def out_copy(l, r):
        return pltpu.make_async_copy(
            S.at[l + 1, rows + r], states_ref.at[l, image_row(r)], out_sem.at[l, r]
        )

    def relaxed_copy(r):
        return pltpu.make_async_copy(
            S.at[layers, rows + r], relaxed_ref.at[0, image_row(r)], relaxed_sem.at[r]
        )

    def put(h, slot, row, v):
        start, width = windows[h]
        column = lax.broadcasted_iota(jnp.int32, (width, chans), 0)
        left = pltpu.roll(v, 1, 0)
        right = pltpu.roll(v, width - 1, 0)
        if h != 0:
            right = jnp.where(column == width - 1, 0.0, right)
        if h != 1:
            left = jnp.where(column == 0, 0.0, left)
            X[slot, row, 0, pl.ds(start, width)] = left.astype(BF16)
        else:
            held = X[slot, row, 0, pl.ds(start, 16)].astype(F32)
            edge = jnp.where(column[:16] == 0, held, left[:16])
            X[slot, row, 0, pl.ds(start, 16)] = edge.astype(BF16)
            X[slot, row, 0, pl.ds(start + 16, width - 16)] = left[16:].astype(BF16)
        X[slot, row, 1, pl.ds(start, width)] = v.astype(BF16)
        X[slot, row, 2, pl.ds(start, width)] = right.astype(BF16)

    none = jnp.zeros((chans, chans), BF16)

    def step(late, h, k, starts):
        start, width = windows[h]
        cut = pl.ds(start, width)
        weights, l = (wf, ws)[1 - k % 2], (k + 1) // 2
        index = l - 1 - late
        weight = pair_weight(
            lambda a, b: weights[index, 3 * (a + flip * (2 - 2 * a)) + b], none
        )
        for g in range(0, len(starts), 2):
            group = starts[g : g + 2]
            lhs = jnp.concatenate(
                [
                    jnp.concatenate(
                        [X[k - 1, r + j - 1, b, cut] for j in range(4) for b in range(3)], axis=1
                    )
                    for r in group
                ],
                axis=0,
            )
            out = jnp.tanh(jnp.dot(lhs, weight, preferred_element_type=F32))
            for n, first in enumerate(group):
                for j in range(2):
                    row = first + j
                    v = out[n * width : (n + 1) * width, j * chans : (j + 1) * chans]
                    if k % 2 == 0:
                        v = S[l - 1, row, cut] + 0.5 * v
                        S[l, row, cut] = v
                    if k < convs:
                        put(h, k, row, v if row < far else jnp.where(inside, v, 0.0))

    def low(k):
        return rows - layers + k if k <= layers else k

    def landed(ref, i, late, h, r):
        if late:
            halves = [ref[i, n, r, pl.ds(0, part)] for n in range(2)]
            return jnp.concatenate(halves, axis=0).astype(F32)
        return ref[i, h, r, pl.ds(0, windows[h][1])].astype(F32)

    def fill(late, h, row, v):
        S[late, row, pl.ds(*windows[h])] = v
        put(h, 2 * late, row, v)

    def own_rows(late, h):
        for r in range(rows):
            put(h, 2 * late, rows + r, S[late, rows + r, pl.ds(*windows[h])])

    def pair_rows(i, late, h):
        for n in range(2) if late else (h,):
            pair_copy(i, late, n).wait_recv()
        for r in range(entry(late)):
            fill(late, h, rows - 1 - r, landed(pair_in, i, late, h, r))

    def edge_rows(i, late, h):
        @pl.when(inside)
        def _():
            for n in range(2) if late else (h,):
                for piece in range(2):
                    edge_copy(i, late, n, piece).wait_recv()

        for r in range(2 * late, rows):
            v = jnp.where(inside, landed(edge_in, i, late, h, r), 0.0)
            fill(late, h, far + rows - 1 - r, v)

    def mid_share(i, late, h):
        start, width = windows[h]
        step(late, h, layers, range(rows, rows + layers, 2))
        for r in range(layers):
            mid_out[h % 2, r, pl.ds(0, width)] = X[layers, rows + r, 1, pl.ds(start, width)]
        mid_copy(i, h).start()

    def mid_rows(i, h):
        start, width = windows[h]
        mid_copy(i, h).wait()
        for r in range(layers):
            v = mid_in[i, h % 2, r, pl.ds(0, width)].astype(F32)
            S[layers // 2, rows - 1 - r, pl.ds(start, width)] = v
            put(h, layers, rows - 1 - r, v)

    def state_out(late, k):
        if late and k % 2 == 0:
            for r in range(rows):
                out_copy(k // 2 - 1, r).start()

    split = low(layers + 1) + layers + 2

    def near(i, late, h):
        own_rows(late, h)
        for k in range(1 + 2 * late, layers):
            step(late, h, k, range(rows + k - 2 * late, far - k, 2))
        pair_rows(i, late, h)
        for k in range(1 + 2 * late, layers):
            step(late, h, k, range(low(k), rows + k - 2 * late, 2))
        mid_share(i, late, h)

    def rest(i, late, h):
        edge_rows(i, late, h)
        for k in range(1 + 2 * late, layers + 1):
            step(late, h, k, range(far - k, far + rows - k, 2))
        state_out(late, layers)
        step(late, h, layers + 1, range(split, far + rows - layers - 1, 2))
        mid_rows(i, h)
        step(late, h, layers + 1, range(low(layers + 1), split, 2))
        last(late, h, layers + 2)

    def joined(i, late, h):
        own_rows(late, h)
        pair_rows(i, late, h)
        edge_rows(i, late, h)
        for k in range(1 + 2 * late, layers - 1):
            step(late, h, k, range(low(k), far + rows - k, 2))
        k = layers - 1
        step(late, h, k, range(low(k), far - k, 2))
        mid_share(i, late, h)
        step(late, h, k, range(far - k, far + rows - k, 2))
        step(late, h, layers, range(rows + layers, far + rows - layers, 2))
        for k in (layers + 1, layers + 2):
            step(late, h, k, range(split + k - layers - 1, far + rows - k, 2))
        mid_rows(i, h)
        for k in (layers + 1, layers + 2):
            step(late, h, k, range(low(k), split + k - layers - 1, 2))
        last(late, h, layers + 3)

    def last(late, h, first):
        for k in range(first, convs):
            step(late, h, k, range(low(k), far + rows - k, 2))
            state_out(late, k)
        step(late, h, convs, range(rows, far, 2))
        state_out(late, convs)

    def sent(i, h):
        @pl.when(i == 0)
        def _():
            start, width = windows[h]
            for r in range(rows):
                ybuf[h, r, pl.ds(0, width)] = S[layers, rows + r, pl.ds(start, width)].astype(BF16)

            @pl.when(d < depths - 1)
            def _():
                for piece in range(2):
                    y_copy(h, piece).start()

        @pl.when(i == 1)
        def _():
            cut = pl.ds(h * part, part)
            for r in range(rows):
                q = S[layers, rows + r, cut] - ybuf[h, r, pl.ds(0, part)].astype(F32)
                qsend[r, cut] = q.astype(BF16)
                scan_copy(0, r, h, qsend, qrecv, partner).start()
            if h == 1:
                for r in range(rows):
                    relaxed_copy(r).start()

    def shifted(h):
        start, width = windows[h]
        for piece in range(2):
            which = range(piece * half, (piece + 1) * half)

            @pl.when(d > 0)
            def _():
                y_copy(h, piece).wait_recv()
                for r in which:
                    S[0, rows + r, pl.ds(start, width)] = own[1, h, r, pl.ds(0, width)].astype(F32)

            @pl.when(d == 0)
            def _():
                for r in which:
                    own[1, h, r, pl.ds(0, width)] = own[0, h, r, pl.ds(0, width)]

            share(1, 0, h, piece)

    def corrected(h, piece):
        for r in range(piece * half, (piece + 1) * half):
            own[2, h, r, pl.ds(0, part)] = S[1, rows + r, pl.ds(h * part, part)].astype(BF16)
        share(2, 1, h, piece)

    def chain(h):
        even = d - odd
        gain_odd = gains[pl.ds((even + 1) % depths, 1), :]
        gain_next = gains[pl.ds((even + 2) % depths, 1), :]
        cut = pl.ds(h * part, part)
        for r in range(rows):
            own_q = S[layers, rows + r, cut] - ybuf[h, r, pl.ds(0, part)].astype(F32)
            scan_copy(0, r, h, qsend, qrecv, partner).wait_recv()
            other = qrecv[r, cut].astype(F32)
            q_even = jnp.where(odd == 0, own_q, other)
            q_odd = jnp.where(odd == 0, other, own_q)

            @pl.when(d > 1)
            def _():
                scan_copy(1, r, h, tsend, trecv, d + 2).wait_recv()

            e_even = trecv[r, cut].astype(F32)
            e_odd = gain_odd * e_even + q_even

            @pl.when(d < depths - 2)
            def _():
                tsend[r, cut] = (gain_next * e_odd + q_odd).astype(BF16)
                scan_copy(1, r, h, tsend, trecv, d + 2).start()

            S[1, rows + r, cut] = S[0, rows + r, cut] + jnp.where(odd == 0, e_even, e_odd)
            if r % half == half - 1:
                corrected(h, r // half)

    @pl.when(jnp.logical_not(inside))
    def _():
        edge_in[...] = jnp.zeros_like(edge_in)

    @pl.when(d < 2)
    def _():
        trecv[...] = jnp.zeros_like(trecv)

    for r in range(rows):
        start_copy(r).wait()
    for h in range(2):
        start, width = windows[h]
        for r in range(rows):
            own[0, h, r, pl.ds(0, width)] = S[0, rows + r, pl.ds(start, width)].astype(BF16)
        for piece in (1, 0):
            share(0, 0, h, piece)
    for l in range(layers):
        for n in range(2):
            weight_copy(n, l).wait()
    gain_copy.wait()

    def sweep(i, carry):
        for h in range(2):

            @pl.when(i == 1)
            def _():
                shifted(h)

            if h == 0:
                near(i, 0, 0)
        rest(i, 0, 0)
        sent(i, 0)
        joined(i, 0, 1)
        sent(i, 1)
        return carry

    lax.fori_loop(0, 2, sweep, 0)

    chain(0)
    chain(1)
    for r in range(rows):
        out_copy(0, r).start()
        relaxed_copy(r).wait()
    near(2, 1, WHOLE)
    rest(2, 1, WHOLE)

    for h in range(2):

        @pl.when(d < depths - 1)
        def _():
            for piece in range(2):
                y_copy(h, piece).wait_send()

        for r in range(rows):
            scan_copy(0, r, h, qsend, qrecv, partner).wait_send()

            @pl.when(d < depths - 2)
            def _():
                scan_copy(1, r, h, tsend, trecv, d + 2).wait_send()

        for i in range(3):
            pair_copy(i, i // 2, h).wait_send()

            @pl.when(inside)
            def _():
                for piece in range(2):
                    edge_copy(i, i // 2, h, piece).wait_send()

    for l in range(layers):
        for r in range(rows):
            out_copy(l, r).wait()


def write_kernel(states_ref, relaxed_ref, states_out, relaxed_out, held, in_sem, out_sem):
    layers = states_ref.shape[0]
    places = [(states_ref, states_out, l, l) for l in range(layers)]
    places.append((relaxed_ref, relaxed_out, 0, layers))
    reads, writes = [], []
    for src, dst, n, at in places:
        reads.append(pltpu.make_async_copy(src.at[n], held.at[at], in_sem.at[at]))
        writes.append(pltpu.make_async_copy(held.at[at], dst.at[n], out_sem.at[at]))
    for copy in reads:
        copy.start()
    for read, write in zip(reads, writes):
        read.wait()
        write.start()
    for copy in writes:
        copy.wait()


def shards(depths, spaces, coarse_states, first_kernels, second_kernels, coarse_channel_gain):
    layers, taps, chans, _ = first_kernels.shape
    _, rows, cols, _ = coarse_states.shape
    assert rows == 2 * layers and layers == 4 and spaces % 2 == 0 and depths % 2 == 0
    wide = column_windows(cols)[0][1]
    hbm = pl.BlockSpec(memory_space=pltpu.HBM)
    field = pltpu.VMEM((rows, cols, chans), BF16)
    slabs = pltpu.VMEM((3, 2, rows, wide, chans), BF16)
    few = pltpu.VMEM((3, 2, layers, wide, chans), BF16)
    mids = pltpu.VMEM((3, 2, layers, cols, chans), BF16)
    dma = pltpu.SemaphoreType.DMA
    results = (
        jax.ShapeDtypeStruct((layers, rows, cols, chans), F32),
        jax.ShapeDtypeStruct((1, rows, cols, chans), F32),
    )
    states, relaxed = pl.pallas_call(
        functools.partial(cycle_kernel, depths, spaces),
        out_shape=results,
        in_specs=[hbm] * 4,
        out_specs=(hbm, hbm),
        scratch_shapes=[
            pltpu.VMEM((layers, taps, chans, chans), BF16),
            pltpu.VMEM((layers, taps, chans, chans), BF16),
            pltpu.VMEM(coarse_channel_gain.shape, F32),
            pltpu.VMEM((2 * layers, 3 * rows, 3, cols, chans), BF16),
            pltpu.VMEM((layers + 1, 3 * rows, cols, chans), F32),
            slabs,
            few,
            mids,
            pltpu.VMEM((2, layers, cols, chans), BF16),
            slabs,
            pltpu.VMEM((2, rows, wide, chans), BF16),
            field,
            field,
            field,
            field,
            dma((rows,)),
            dma((2, layers)),
            dma,
            dma((3, 2)),
            dma((3, 2)),
            dma((3, 2)),
            dma((3, 2)),
            dma((3, 2, 2)),
            dma((3, 2, 2)),
            dma((2, 2)),
            dma((2, 2)),
            dma((2, rows, 2)),
            dma((2, rows, 2)),
            dma((layers, rows)),
            dma((rows,)),
        ],
        compiler_params=pltpu.CompilerParams(
            collective_id=0, has_side_effects=True, vmem_limit_bytes=58 * 1024 * 1024
        ),
    )(coarse_states[0], first_kernels, second_kernels, coarse_channel_gain)
    return pl.pallas_call(
        write_kernel,
        out_shape=results,
        in_specs=[hbm] * 2,
        out_specs=(hbm, hbm),
        scratch_shapes=[
            pltpu.VMEM((layers + 1, rows, cols, chans), F32),
            dma((layers + 1,)),
            dma((layers + 1,)),
        ],
    )(states, relaxed)


def solution(mesh):
    depths, spaces = mesh.shape["depth"], mesh.shape["space"]
    placed = (
        P("depth", "space", None, None),
        P("depth", None, None, None),
        P("depth", None, None, None),
        P(),
    )
    return jax.shard_map(
        functools.partial(shards, depths, spaces),
        mesh=mesh,
        in_specs=placed,
        out_specs=(P("depth", "space", None, None), P("depth", "space", None, None)),
        check_vma=False,
    )
```

```python
import functools

import jax
import jax.numpy as jnp
from jax import lax
from jax.experimental import pallas as pl
from jax.experimental.pallas import tpu as pltpu
from jax.sharding import PartitionSpec as P

MESH = pl.DeviceIdType.MESH
F32 = jnp.float32
BF16 = jnp.bfloat16


def pair_weight(tap, none):
    blocks = []
    for i in range(4):
        for b in range(3):
            one = tap(i, b) if i < 3 else none
            two = tap(i - 1, b) if i > 0 else none
            blocks.append(jnp.concatenate([one, two], axis=1))
    return jnp.concatenate(blocks, axis=0)


def column_windows(cols):
    part, lap = cols // 2, 16
    return (0, part + lap), (part, part), (0, cols)


WHOLE = 2


def cycle_kernel(
    depths,
    spaces,
    start_ref,
    first_ref,
    second_ref,
    gain_ref,
    states_ref,
    relaxed_ref,
    wf,
    ws,
    gains,
    X,
    S,
    own,
    pair_in,
    mid_in,
    mid_out,
    edge_in,
    ybuf,
    qsend,
    qrecv,
    tsend,
    trecv,
    start_sem,
    weight_sem,
    gain_sem,
    pair_send,
    pair_recv,
    mid_send,
    mid_recv,
    edge_send,
    edge_recv,
    y_send,
    y_recv,
    scan_send,
    scan_recv,
    out_sem,
    relaxed_sem,
):
    layers = first_ref.shape[0]
    rows, cols, chans = start_ref.shape
    convs = 2 * layers
    far = 2 * rows
    half = rows // 2
    part = cols // 2
    windows = column_windows(cols)
    d = lax.axis_index("depth")
    s = lax.axis_index("space")
    odd = d % 2
    partner = d + 1 - 2 * odd
    flip = 1 - s % 2
    pair = s + 1 - 2 * (s % 2)
    across = s - 1 + 2 * (s % 2)
    inside = (across >= 0) & (across < spaces)

    def image_row(r):
        return r + flip * (rows - 1 - 2 * r)

    def start_copy(r):
        return pltpu.make_async_copy(
            start_ref.at[image_row(r)], S.at[0, rows + r], start_sem.at[r]
        )

    def weight_copy(n, l):
        src, dst = ((first_ref, wf), (second_ref, ws))[n]
        return pltpu.make_async_copy(src.at[l], dst.at[l], weight_sem.at[n, l])

    for r in range(rows):
        start_copy(r).start()
    for l in range(layers):
        for n in range(2):
            weight_copy(n, l).start()
    gain_copy = pltpu.make_async_copy(gain_ref, gains, gain_sem)
    gain_copy.start()

    barrier = pltpu.get_barrier_semaphore()
    meets = [
        (s > 0, (d, s - 1)),
        (s < spaces - 1, (d, s + 1)),
        (d > 0, (d - 1, s)),
        (d < depths - 1, (d + 1, s)),
        (d > 1, (d - 2, s)),
        (d < depths - 2, (d + 2, s)),
    ]

    def greet(there, device):
        @pl.when(there)
        def _():
            pl.semaphore_signal(barrier, inc=1, device_id=device, device_id_type=MESH)

    for there, device in meets:
        greet(there, device)
    pl.semaphore_wait(barrier, sum(there.astype(jnp.int32) for there, _ in meets))

    def remote(src, dst, sends, recvs, at, device):
        return pltpu.make_async_remote_copy(
            src_ref=src,
            dst_ref=dst,
            send_sem=sends.at[at],
            recv_sem=recvs.at[at],
            device_id=device,
            device_id_type=MESH,
        )

    def entry(late):
        return layers - 2 * late

    def sent_width(late, h):
        return part if late else windows[h][1]

    def pair_copy(i, late, h):
        at = (i, h, pl.ds(0, entry(late)), pl.ds(0, sent_width(late, h)))
        return remote(own.at[at], pair_in.at[at], pair_send, pair_recv, (i, h), (d, pair))

    def mid_copy(i, h):
        n, cut = h % 2, pl.ds(0, windows[h][1])
        return remote(
            mid_out.at[n, :, cut],
            mid_in.at[i, n, :, cut],
            mid_send,
            mid_recv,
            (i, n),
            (d, pair),
        )

    def edge_copy(i, late, h, piece):
        first = 2 * late if piece == 0 else half
        at = (i, h, pl.ds(first, half * (piece + 1) - first), pl.ds(0, sent_width(late, h)))
        return remote(
            own.at[at], edge_in.at[at], edge_send, edge_recv, (i, h, piece), (d, across)
        )

    def share(i, late, h, piece):
        if piece == 0:
            pair_copy(i, late, h).start()

        @pl.when(inside)
        def _():
            edge_copy(i, late, h, piece).start()

    def y_copy(h, piece):
        at = (pl.ds(piece * half, half), pl.ds(0, windows[h][1]))
        return remote(
            ybuf.at[(h,) + at], own.at[(1, h) + at], y_send, y_recv, (h, piece), (d + 1, s)
        )

    def scan_copy(kind, r, h, src, dst, device):
        at = (r, pl.ds(h * part, part))
        return remote(src.at[at], dst.at[at], scan_send, scan_recv, (kind, r, h), (device, s))

    def out_copy(l, r):
        return pltpu.make_async_copy(
            S.at[l + 1, rows + r], states_ref.at[l, image_row(r)], out_sem.at[l, r]
        )

    def relaxed_copy(r):
        return pltpu.make_async_copy(
            S.at[layers, rows + r], relaxed_ref.at[0, image_row(r)], relaxed_sem.at[r]
        )

    def put(h, slot, row, v):
        start, width = windows[h]
        column = lax.broadcasted_iota(jnp.int32, (width, chans), 0)
        left = pltpu.roll(v, 1, 0)
        right = pltpu.roll(v, width - 1, 0)
        if h != 0:
            right = jnp.where(column == width - 1, 0.0, right)
        if h != 1:
            left = jnp.where(column == 0, 0.0, left)
            X[slot, row, 0, pl.ds(start, width)] = left.astype(BF16)
        else:
            held = X[slot, row, 0, pl.ds(start, 16)].astype(F32)
            edge = jnp.where(column[:16] == 0, held, left[:16])
            X[slot, row, 0, pl.ds(start, 16)] = edge.astype(BF16)
            X[slot, row, 0, pl.ds(start + 16, width - 16)] = left[16:].astype(BF16)
        X[slot, row, 1, pl.ds(start, width)] = v.astype(BF16)
        X[slot, row, 2, pl.ds(start, width)] = right.astype(BF16)

    none = jnp.zeros((chans, chans), BF16)

    def step(late, h, k, starts):
        start, width = windows[h]
        cut = pl.ds(start, width)
        weights, l = (wf, ws)[1 - k % 2], (k + 1) // 2
        index = l - 1 - late
        weight = pair_weight(
            lambda a, b: weights[index, 3 * (a + flip * (2 - 2 * a)) + b], none
        )
        size = 1 if h == WHOLE else 2
        for g in range(0, len(starts), size):
            group = starts[g : g + size]
            lhs = jnp.concatenate(
                [
                    jnp.concatenate(
                        [X[k - 1, r + j - 1, b, cut] for j in range(4) for b in range(3)], axis=1
                    )
                    for r in group
                ],
                axis=0,
            )
            out = jnp.tanh(jnp.dot(lhs, weight, preferred_element_type=F32))
            for n, first in enumerate(group):
                for j in range(2):
                    row = first + j
                    v = out[n * width : (n + 1) * width, j * chans : (j + 1) * chans]
                    if k % 2 == 0:
                        v = S[l - 1, row, cut] + 0.5 * v
                        S[l, row, cut] = v
                    if k < convs:
                        put(h, k, row, v if row < far else jnp.where(inside, v, 0.0))

    def low(k):
        return rows - layers + k if k <= layers else k

    def landed(ref, i, late, h, r):
        if late:
            halves = [ref[i, n, r, pl.ds(0, part)] for n in range(2)]
            return jnp.concatenate(halves, axis=0).astype(F32)
        return ref[i, h, r, pl.ds(0, windows[h][1])].astype(F32)

    def fill(late, h, row, v):
        S[late, row, pl.ds(*windows[h])] = v
        put(h, 2 * late, row, v)

    def own_rows(late, h):
        for r in range(rows):
            put(h, 2 * late, rows + r, S[late, rows + r, pl.ds(*windows[h])])

    def pair_rows(i, late, h):
        for n in range(2) if late else (h,):
            pair_copy(i, late, n).wait_recv()
        for r in range(entry(late)):
            fill(late, h, rows - 1 - r, landed(pair_in, i, late, h, r))

    def edge_rows(i, late, h):
        @pl.when(inside)
        def _():
            for n in range(2) if late else (h,):
                for piece in range(2):
                    edge_copy(i, late, n, piece).wait_recv()

        for r in range(2 * late, rows):
            v = jnp.where(inside, landed(edge_in, i, late, h, r), 0.0)
            fill(late, h, far + rows - 1 - r, v)

    def mid_share(i, late, h):
        start, width = windows[h]
        step(late, h, layers, range(rows, rows + layers, 2))
        for r in range(layers):
            mid_out[h % 2, r, pl.ds(0, width)] = X[layers, rows + r, 1, pl.ds(start, width)]
        mid_copy(i, h).start()

    def mid_rows(i, h):
        start, width = windows[h]
        mid_copy(i, h).wait()
        for r in range(layers):
            v = mid_in[i, h % 2, r, pl.ds(0, width)].astype(F32)
            S[layers // 2, rows - 1 - r, pl.ds(start, width)] = v
            put(h, layers, rows - 1 - r, v)

    def state_out(late, k):
        if late and k % 2 == 0:
            for r in range(rows):
                out_copy(k // 2 - 1, r).start()

    split = low(layers + 1) + layers + 2

    def near(i, late, h):
        own_rows(late, h)
        for k in range(1 + 2 * late, layers):
            step(late, h, k, range(rows + k - 2 * late, far - k, 2))
        pair_rows(i, late, h)
        for k in range(1 + 2 * late, layers):
            step(late, h, k, range(low(k), rows + k - 2 * late, 2))
        mid_share(i, late, h)

    def rest(i, late, h):
        edge_rows(i, late, h)
        for k in range(1 + 2 * late, layers + 1):
            step(late, h, k, range(far - k, far + rows - k, 2))
        state_out(late, layers)
        step(late, h, layers + 1, range(split, far + rows - layers - 1, 2))
        mid_rows(i, h)
        step(late, h, layers + 1, range(low(layers + 1), split, 2))
        last(late, h, layers + 2)

    def joined(i, late, h):
        own_rows(late, h)
        pair_rows(i, late, h)
        edge_rows(i, late, h)
        for k in range(1 + 2 * late, layers - 1):
            step(late, h, k, range(low(k), far + rows - k, 2))
        k = layers - 1
        step(late, h, k, range(low(k), far - k, 2))
        mid_share(i, late, h)
        step(late, h, k, range(far - k, far + rows - k, 2))
        step(late, h, layers, range(rows + layers, far + rows - layers, 2))
        for k in (layers + 1, layers + 2):
            step(late, h, k, range(split + k - layers - 1, far + rows - k, 2))
        mid_rows(i, h)
        for k in (layers + 1, layers + 2):
            step(late, h, k, range(low(k), split + k - layers - 1, 2))
        last(late, h, layers + 3)

    def last(late, h, first):
        for k in range(first, convs):
            step(late, h, k, range(low(k), far + rows - k, 2))
            state_out(late, k)
        step(late, h, convs, range(rows, far, 2))
        state_out(late, convs)

    def sent(i, h):
        @pl.when(i == 0)
        def _():
            start, width = windows[h]
            for r in range(rows):
                ybuf[h, r, pl.ds(0, width)] = S[layers, rows + r, pl.ds(start, width)].astype(BF16)

            @pl.when(d < depths - 1)
            def _():
                for piece in range(2):
                    y_copy(h, piece).start()

        @pl.when(i == 1)
        def _():
            cut = pl.ds(h * part, part)
            for r in range(rows):
                q = S[layers, rows + r, cut] - ybuf[h, r, pl.ds(0, part)].astype(F32)
                qsend[r, cut] = q.astype(BF16)
                scan_copy(0, r, h, qsend, qrecv, partner).start()
            if h == 1:
                for r in range(rows):
                    relaxed_copy(r).start()

    def shifted(h):
        start, width = windows[h]
        for piece in range(2):
            which = range(piece * half, (piece + 1) * half)

            @pl.when(d > 0)
            def _():
                y_copy(h, piece).wait_recv()
                for r in which:
                    S[0, rows + r, pl.ds(start, width)] = own[1, h, r, pl.ds(0, width)].astype(F32)

            @pl.when(d == 0)
            def _():
                for r in which:
                    own[1, h, r, pl.ds(0, width)] = own[0, h, r, pl.ds(0, width)]

            share(1, 0, h, piece)

    def corrected(h, piece):
        for r in range(piece * half, (piece + 1) * half):
            own[2, h, r, pl.ds(0, part)] = S[1, rows + r, pl.ds(h * part, part)].astype(BF16)
        share(2, 1, h, piece)

    def chain(h):
        even = d - odd
        gain_odd = gains[pl.ds((even + 1) % depths, 1), :]
        gain_next = gains[pl.ds((even + 2) % depths, 1), :]
        cut = pl.ds(h * part, part)
        for r in range(rows):
            own_q = S[layers, rows + r, cut] - ybuf[h, r, pl.ds(0, part)].astype(F32)
            scan_copy(0, r, h, qsend, qrecv, partner).wait_recv()
            other = qrecv[r, cut].astype(F32)
            q_even = jnp.where(odd == 0, own_q, other)
            q_odd = jnp.where(odd == 0, other, own_q)

            @pl.when(d > 1)
            def _():
                scan_copy(1, r, h, tsend, trecv, d + 2).wait_recv()

            e_even = trecv[r, cut].astype(F32)
            e_odd = gain_odd * e_even + q_even

            @pl.when(d < depths - 2)
            def _():
                tsend[r, cut] = (gain_next * e_odd + q_odd).astype(BF16)
                scan_copy(1, r, h, tsend, trecv, d + 2).start()

            S[1, rows + r, cut] = S[0, rows + r, cut] + jnp.where(odd == 0, e_even, e_odd)
            if r % half == half - 1:
                corrected(h, r // half)

    @pl.when(jnp.logical_not(inside))
    def _():
        edge_in[...] = jnp.zeros_like(edge_in)

    @pl.when(d < 2)
    def _():
        trecv[...] = jnp.zeros_like(trecv)

    for r in range(rows):
        start_copy(r).wait()
    for h in range(2):
        start, width = windows[h]
        for r in range(rows):
            own[0, h, r, pl.ds(0, width)] = S[0, rows + r, pl.ds(start, width)].astype(BF16)
        for piece in (1, 0):
            share(0, 0, h, piece)
    for l in range(layers):
        for n in range(2):
            weight_copy(n, l).wait()
    gain_copy.wait()

    def sweep(i, carry):
        for h in range(2):

            @pl.when(i == 1)
            def _():
                shifted(h)

            if h == 0:
                near(i, 0, 0)
        rest(i, 0, 0)
        sent(i, 0)
        joined(i, 0, 1)
        sent(i, 1)
        return carry

    lax.fori_loop(0, 2, sweep, 0)

    chain(0)
    chain(1)
    for r in range(rows):
        out_copy(0, r).start()
        relaxed_copy(r).wait()
    near(2, 1, WHOLE)
    rest(2, 1, WHOLE)

    for h in range(2):

        @pl.when(d < depths - 1)
        def _():
            for piece in range(2):
                y_copy(h, piece).wait_send()

        for r in range(rows):
            scan_copy(0, r, h, qsend, qrecv, partner).wait_send()

            @pl.when(d < depths - 2)
            def _():
                scan_copy(1, r, h, tsend, trecv, d + 2).wait_send()

        for i in range(3):
            pair_copy(i, i // 2, h).wait_send()

            @pl.when(inside)
            def _():
                for piece in range(2):
                    edge_copy(i, i // 2, h, piece).wait_send()

    for l in range(layers):
        for r in range(rows):
            out_copy(l, r).wait()


def write_kernel(states_ref, relaxed_ref, states_out, relaxed_out, held, in_sem, out_sem):
    layers = states_ref.shape[0]
    places = [(states_ref, states_out, l, l) for l in range(layers)]
    places.append((relaxed_ref, relaxed_out, 0, layers))
    reads, writes = [], []
    for src, dst, n, at in places:
        reads.append(pltpu.make_async_copy(src.at[n], held.at[at], in_sem.at[at]))
        writes.append(pltpu.make_async_copy(held.at[at], dst.at[n], out_sem.at[at]))
    for copy in reads:
        copy.start()
    for read, write in zip(reads, writes):
        read.wait()
        write.start()
    for copy in writes:
        copy.wait()


def shards(depths, spaces, coarse_states, first_kernels, second_kernels, coarse_channel_gain):
    layers, taps, chans, _ = first_kernels.shape
    _, rows, cols, _ = coarse_states.shape
    assert rows == 2 * layers and layers == 4 and spaces % 2 == 0 and depths % 2 == 0
    wide = column_windows(cols)[0][1]
    hbm = pl.BlockSpec(memory_space=pltpu.HBM)
    field = pltpu.VMEM((rows, cols, chans), BF16)
    slabs = pltpu.VMEM((3, 2, rows, wide, chans), BF16)
    few = pltpu.VMEM((3, 2, layers, wide, chans), BF16)
    mids = pltpu.VMEM((3, 2, layers, cols, chans), BF16)
    dma = pltpu.SemaphoreType.DMA
    results = (
        jax.ShapeDtypeStruct((layers, rows, cols, chans), F32),
        jax.ShapeDtypeStruct((1, rows, cols, chans), F32),
    )
    states, relaxed = pl.pallas_call(
        functools.partial(cycle_kernel, depths, spaces),
        out_shape=results,
        in_specs=[hbm] * 4,
        out_specs=(hbm, hbm),
        scratch_shapes=[
            pltpu.VMEM((layers, taps, chans, chans), BF16),
            pltpu.VMEM((layers, taps, chans, chans), BF16),
            pltpu.VMEM(coarse_channel_gain.shape, F32),
            pltpu.VMEM((2 * layers, 3 * rows, 3, cols, chans), BF16),
            pltpu.VMEM((layers + 1, 3 * rows, cols, chans), F32),
            slabs,
            few,
            mids,
            pltpu.VMEM((2, layers, cols, chans), BF16),
            slabs,
            pltpu.VMEM((2, rows, wide, chans), BF16),
            field,
            field,
            field,
            field,
            dma((rows,)),
            dma((2, layers)),
            dma,
            dma((3, 2)),
            dma((3, 2)),
            dma((3, 2)),
            dma((3, 2)),
            dma((3, 2, 2)),
            dma((3, 2, 2)),
            dma((2, 2)),
            dma((2, 2)),
            dma((2, rows, 2)),
            dma((2, rows, 2)),
            dma((layers, rows)),
            dma((rows,)),
        ],
        compiler_params=pltpu.CompilerParams(
            collective_id=0, has_side_effects=True, vmem_limit_bytes=58 * 1024 * 1024
        ),
    )(coarse_states[0], first_kernels, second_kernels, coarse_channel_gain)
    return pl.pallas_call(
        write_kernel,
        out_shape=results,
        in_specs=[hbm] * 2,
        out_specs=(hbm, hbm),
        scratch_shapes=[
            pltpu.VMEM((layers + 1, rows, cols, chans), F32),
            dma((layers + 1,)),
            dma((layers + 1,)),
        ],
    )(states, relaxed)


def solution(mesh):
    depths, spaces = mesh.shape["depth"], mesh.shape["space"]
    placed = (
        P("depth", "space", None, None),
        P("depth", None, None, None),
        P("depth", None, None, None),
        P(),
    )
    return jax.shard_map(
        functools.partial(shards, depths, spaces),
        mesh=mesh,
        in_specs=placed,
        out_specs=(P("depth", "space", None, None), P("depth", "space", None, None)),
        check_vma=False,
    )
```

```python
import functools

import jax
import jax.numpy as jnp
from jax import lax
from jax.experimental import pallas as pl
from jax.experimental.pallas import tpu as pltpu
from jax.sharding import PartitionSpec as P

MESH = pl.DeviceIdType.MESH
F32 = jnp.float32
BF16 = jnp.bfloat16


def pair_weight(tap, none):
    blocks = []
    for i in range(4):
        for b in range(3):
            one = tap(i, b) if i < 3 else none
            two = tap(i - 1, b) if i > 0 else none
            blocks.append(jnp.concatenate([one, two], axis=1))
    return jnp.concatenate(blocks, axis=0)


def column_windows(cols):
    part, lap = cols // 2, 16
    return (0, part + lap), (part, part), (0, cols)


WHOLE = 2


def cycle_kernel(
    depths,
    spaces,
    start_ref,
    first_ref,
    second_ref,
    gain_ref,
    states_ref,
    relaxed_ref,
    wf,
    ws,
    gains,
    X,
    S,
    own,
    pair_in,
    mid_in,
    mid_out,
    edge_in,
    ybuf,
    qsend,
    qrecv,
    tsend,
    trecv,
    start_sem,
    weight_sem,
    gain_sem,
    pair_send,
    pair_recv,
    mid_send,
    mid_recv,
    edge_send,
    edge_recv,
    y_send,
    y_recv,
    scan_send,
    scan_recv,
    out_sem,
    relaxed_sem,
):
    layers = first_ref.shape[0]
    rows, cols, chans = start_ref.shape
    convs = 2 * layers
    far = 2 * rows
    half = rows // 2
    part = cols // 2
    windows = column_windows(cols)
    d = lax.axis_index("depth")
    s = lax.axis_index("space")
    odd = d % 2
    partner = d + 1 - 2 * odd
    flip = 1 - s % 2
    pair = s + 1 - 2 * (s % 2)
    across = s - 1 + 2 * (s % 2)
    inside = (across >= 0) & (across < spaces)

    def image_row(r):
        return r + flip * (rows - 1 - 2 * r)

    def start_copy(r):
        return pltpu.make_async_copy(
            start_ref.at[image_row(r)], S.at[0, rows + r], start_sem.at[r]
        )

    def weight_copy(n, l):
        src, dst = ((first_ref, wf), (second_ref, ws))[n]
        return pltpu.make_async_copy(src.at[l], dst.at[l], weight_sem.at[n, l])

    for r in range(rows):
        start_copy(r).start()
    for l in range(layers):
        for n in range(2):
            weight_copy(n, l).start()
    gain_copy = pltpu.make_async_copy(gain_ref, gains, gain_sem)
    gain_copy.start()

    barrier = pltpu.get_barrier_semaphore()
    meets = [
        (s > 0, (d, s - 1)),
        (s < spaces - 1, (d, s + 1)),
        (d > 0, (d - 1, s)),
        (d < depths - 1, (d + 1, s)),
        (d > 1, (d - 2, s)),
        (d < depths - 2, (d + 2, s)),
    ]

    def greet(there, device):
        @pl.when(there)
        def _():
            pl.semaphore_signal(barrier, inc=1, device_id=device, device_id_type=MESH)

    for there, device in meets:
        greet(there, device)

    def remote(src, dst, sends, recvs, at, device):
        return pltpu.make_async_remote_copy(
            src_ref=src,
            dst_ref=dst,
            send_sem=sends.at[at],
            recv_sem=recvs.at[at],
            device_id=device,
            device_id_type=MESH,
        )

    def entry(late):
        return layers - 2 * late

    def sent_width(late, h):
        return part if late else windows[h][1]

    def pair_copy(i, late, h):
        at = (i, h, pl.ds(0, entry(late)), pl.ds(0, sent_width(late, h)))
        return remote(own.at[at], pair_in.at[at], pair_send, pair_recv, (i, h), (d, pair))

    def mid_copy(i, h):
        n, cut = h % 2, pl.ds(0, windows[h][1])
        return remote(
            mid_out.at[n, :, cut],
            mid_in.at[i, n, :, cut],
            mid_send,
            mid_recv,
            (i, n),
            (d, pair),
        )

    def edge_copy(i, late, h, piece):
        first = 2 * late if piece == 0 else half
        at = (i, h, pl.ds(first, half * (piece + 1) - first), pl.ds(0, sent_width(late, h)))
        return remote(
            own.at[at], edge_in.at[at], edge_send, edge_recv, (i, h, piece), (d, across)
        )

    def share(i, late, h, piece):
        if piece == 0:
            pair_copy(i, late, h).start()

        @pl.when(inside)
        def _():
            edge_copy(i, late, h, piece).start()

    def y_copy(h, piece):
        at = (pl.ds(piece * half, half), pl.ds(0, windows[h][1]))
        return remote(
            ybuf.at[(h,) + at], own.at[(1, h) + at], y_send, y_recv, (h, piece), (d + 1, s)
        )

    def scan_copy(kind, r, h, src, dst, device):
        at = (r, pl.ds(h * part, part))
        return remote(src.at[at], dst.at[at], scan_send, scan_recv, (kind, r, h), (device, s))

    def out_copy(l, r):
        return pltpu.make_async_copy(
            S.at[l + 1, rows + r], states_ref.at[l, image_row(r)], out_sem.at[l, r]
        )

    def relaxed_copy(r):
        return pltpu.make_async_copy(
            S.at[layers, rows + r], relaxed_ref.at[0, image_row(r)], relaxed_sem.at[r]
        )

    def put(h, slot, row, v):
        start, width = windows[h]
        column = lax.broadcasted_iota(jnp.int32, (width, chans), 0)
        left = pltpu.roll(v, 1, 0)
        right = pltpu.roll(v, width - 1, 0)
        if h != 0:
            right = jnp.where(column == width - 1, 0.0, right)
        if h != 1:
            left = jnp.where(column == 0, 0.0, left)
            X[slot, row, 0, pl.ds(start, width)] = left.astype(BF16)
        else:
            held = X[slot, row, 0, pl.ds(start, 16)].astype(F32)
            edge = jnp.where(column[:16] == 0, held, left[:16])
            X[slot, row, 0, pl.ds(start, 16)] = edge.astype(BF16)
            X[slot, row, 0, pl.ds(start + 16, width - 16)] = left[16:].astype(BF16)
        X[slot, row, 1, pl.ds(start, width)] = v.astype(BF16)
        X[slot, row, 2, pl.ds(start, width)] = right.astype(BF16)

    none = jnp.zeros((chans, chans), BF16)

    def step(late, h, k, starts):
        start, width = windows[h]
        cut = pl.ds(start, width)
        weights, l = (wf, ws)[1 - k % 2], (k + 1) // 2
        index = l - 1 - late
        weight = pair_weight(
            lambda a, b: weights[index, 3 * (a + flip * (2 - 2 * a)) + b], none
        )
        size = 1 if h == WHOLE else 2
        for g in range(0, len(starts), size):
            group = starts[g : g + size]
            lhs = jnp.concatenate(
                [
                    jnp.concatenate(
                        [X[k - 1, r + j - 1, b, cut] for j in range(4) for b in range(3)], axis=1
                    )
                    for r in group
                ],
                axis=0,
            )
            out = jnp.tanh(jnp.dot(lhs, weight, preferred_element_type=F32))
            for n, first in enumerate(group):
                for j in range(2):
                    row = first + j
                    v = out[n * width : (n + 1) * width, j * chans : (j + 1) * chans]
                    if k % 2 == 0:
                        v = S[l - 1, row, cut] + 0.5 * v
                        S[l, row, cut] = v
                    if k < convs:
                        put(h, k, row, v if row < far else jnp.where(inside, v, 0.0))

    def low(k):
        return rows - layers + k if k <= layers else k

    def landed(ref, i, late, h, r):
        if late:
            halves = [ref[i, n, r, pl.ds(0, part)] for n in range(2)]
            return jnp.concatenate(halves, axis=0).astype(F32)
        return ref[i, h, r, pl.ds(0, windows[h][1])].astype(F32)

    def fill(late, h, row, v):
        S[late, row, pl.ds(*windows[h])] = v
        put(h, 2 * late, row, v)

    def own_rows(late, h):
        for r in range(rows):
            put(h, 2 * late, rows + r, S[late, rows + r, pl.ds(*windows[h])])

    def pair_rows(i, late, h):
        for n in range(2) if late else (h,):
            pair_copy(i, late, n).wait_recv()
        for r in range(entry(late)):
            fill(late, h, rows - 1 - r, landed(pair_in, i, late, h, r))

    def edge_rows(i, late, h):
        @pl.when(inside)
        def _():
            for n in range(2) if late else (h,):
                for piece in range(2):
                    edge_copy(i, late, n, piece).wait_recv()

        for r in range(2 * late, rows):
            v = jnp.where(inside, landed(edge_in, i, late, h, r), 0.0)
            fill(late, h, far + rows - 1 - r, v)

    def mid_share(i, late, h):
        start, width = windows[h]
        step(late, h, layers, range(rows, rows + layers, 2))
        for r in range(layers):
            mid_out[h % 2, r, pl.ds(0, width)] = X[layers, rows + r, 1, pl.ds(start, width)]
        mid_copy(i, h).start()

    def mid_rows(i, h):
        start, width = windows[h]
        mid_copy(i, h).wait()
        for r in range(layers):
            v = mid_in[i, h % 2, r, pl.ds(0, width)].astype(F32)
            S[layers // 2, rows - 1 - r, pl.ds(start, width)] = v
            put(h, layers, rows - 1 - r, v)

    def state_out(late, k):
        if late and k % 2 == 0:
            for r in range(rows):
                out_copy(k // 2 - 1, r).start()

    split = low(layers + 1) + layers + 2

    def near(i, late, h):
        own_rows(late, h)
        for k in range(1 + 2 * late, layers):
            step(late, h, k, range(rows + k - 2 * late, far - k, 2))
        pair_rows(i, late, h)
        for k in range(1 + 2 * late, layers):
            step(late, h, k, range(low(k), rows + k - 2 * late, 2))
        mid_share(i, late, h)

    def rest(i, late, h):
        edge_rows(i, late, h)
        for k in range(1 + 2 * late, layers + 1):
            step(late, h, k, range(far - k, far + rows - k, 2))
        state_out(late, layers)
        step(late, h, layers + 1, range(split, far + rows - layers - 1, 2))
        mid_rows(i, h)
        step(late, h, layers + 1, range(low(layers + 1), split, 2))
        last(late, h, layers + 2)

    def joined(i, late, h):
        own_rows(late, h)
        pair_rows(i, late, h)
        edge_rows(i, late, h)
        for k in range(1 + 2 * late, layers - 1):
            step(late, h, k, range(low(k), far + rows - k, 2))
        k = layers - 1
        step(late, h, k, range(low(k), far - k, 2))
        mid_share(i, late, h)
        step(late, h, k, range(far - k, far + rows - k, 2))
        step(late, h, layers, range(rows + layers, far + rows - layers, 2))
        for k in (layers + 1, layers + 2):
            step(late, h, k, range(split + k - layers - 1, far + rows - k, 2))
        mid_rows(i, h)
        for k in (layers + 1, layers + 2):
            step(late, h, k, range(low(k), split + k - layers - 1, 2))
        last(late, h, layers + 3)

    def last(late, h, first):
        for k in range(first, convs):
            step(late, h, k, range(low(k), far + rows - k, 2))
            state_out(late, k)
        step(late, h, convs, range(rows, far, 2))
        state_out(late, convs)

    def sent(i, h):
        @pl.when(i == 0)
        def _():
            start, width = windows[h]
            for r in range(rows):
                ybuf[h, r, pl.ds(0, width)] = S[layers, rows + r, pl.ds(start, width)].astype(BF16)

            @pl.when(d < depths - 1)
            def _():
                for piece in range(2):
                    y_copy(h, piece).start()

        @pl.when(i == 1)
        def _():
            cut = pl.ds(h * part, part)
            for r in range(rows):
                q = S[layers, rows + r, cut] - ybuf[h, r, pl.ds(0, part)].astype(F32)
                qsend[r, cut] = q.astype(BF16)
                scan_copy(0, r, h, qsend, qrecv, partner).start()
            if h == 1:
                for r in range(rows):
                    relaxed_copy(r).start()

    def shifted(h):
        start, width = windows[h]
        for piece in range(2):
            which = range(piece * half, (piece + 1) * half)

            @pl.when(d > 0)
            def _():
                y_copy(h, piece).wait_recv()
                for r in which:
                    S[0, rows + r, pl.ds(start, width)] = own[1, h, r, pl.ds(0, width)].astype(F32)

            @pl.when(d == 0)
            def _():
                for r in which:
                    own[1, h, r, pl.ds(0, width)] = own[0, h, r, pl.ds(0, width)]

            share(1, 0, h, piece)

    def corrected(h, piece):
        for r in range(piece * half, (piece + 1) * half):
            own[2, h, r, pl.ds(0, part)] = S[1, rows + r, pl.ds(h * part, part)].astype(BF16)
        share(2, 1, h, piece)

    def chain(h):
        even = d - odd
        gain_odd = gains[pl.ds((even + 1) % depths, 1), :]
        gain_next = gains[pl.ds((even + 2) % depths, 1), :]
        cut = pl.ds(h * part, part)
        for r in range(rows):
            own_q = S[layers, rows + r, cut] - ybuf[h, r, pl.ds(0, part)].astype(F32)
            scan_copy(0, r, h, qsend, qrecv, partner).wait_recv()
            other = qrecv[r, cut].astype(F32)
            q_even = jnp.where(odd == 0, own_q, other)
            q_odd = jnp.where(odd == 0, other, own_q)

            @pl.when(d > 1)
            def _():
                scan_copy(1, r, h, tsend, trecv, d + 2).wait_recv()

            e_even = trecv[r, cut].astype(F32)
            e_odd = gain_odd * e_even + q_even

            @pl.when(d < depths - 2)
            def _():
                tsend[r, cut] = (gain_next * e_odd + q_odd).astype(BF16)
                scan_copy(1, r, h, tsend, trecv, d + 2).start()

            S[1, rows + r, cut] = S[0, rows + r, cut] + jnp.where(odd == 0, e_even, e_odd)
            if r % half == half - 1:
                corrected(h, r // half)

    @pl.when(jnp.logical_not(inside))
    def _():
        edge_in[...] = jnp.zeros_like(edge_in)

    @pl.when(d < 2)
    def _():
        trecv[...] = jnp.zeros_like(trecv)

    for r in range(rows):
        start_copy(r).wait()
    for h in range(2):
        start, width = windows[h]
        for r in range(rows):
            own[0, h, r, pl.ds(0, width)] = S[0, rows + r, pl.ds(start, width)].astype(BF16)
    pl.semaphore_wait(barrier, sum(there.astype(jnp.int32) for there, _ in meets))
    for h in range(2):
        for piece in (1, 0):
            share(0, 0, h, piece)
    for l in range(layers):
        for n in range(2):
            weight_copy(n, l).wait()
    gain_copy.wait()

    def sweep(i, carry):
        for h in range(2):

            @pl.when(i == 1)
            def _():
                shifted(h)

            if h == 0:
                near(i, 0, 0)
        rest(i, 0, 0)
        sent(i, 0)
        joined(i, 0, 1)
        sent(i, 1)
        return carry

    lax.fori_loop(0, 2, sweep, 0)

    chain(0)
    chain(1)
    for r in range(rows):
        out_copy(0, r).start()
        relaxed_copy(r).wait()
    near(2, 1, WHOLE)
    rest(2, 1, WHOLE)

    for h in range(2):

        @pl.when(d < depths - 1)
        def _():
            for piece in range(2):
                y_copy(h, piece).wait_send()

        for r in range(rows):
            scan_copy(0, r, h, qsend, qrecv, partner).wait_send()

            @pl.when(d < depths - 2)
            def _():
                scan_copy(1, r, h, tsend, trecv, d + 2).wait_send()

        for i in range(3):
            pair_copy(i, i // 2, h).wait_send()

            @pl.when(inside)
            def _():
                for piece in range(2):
                    edge_copy(i, i // 2, h, piece).wait_send()

    for l in range(layers):
        for r in range(rows):
            out_copy(l, r).wait()


def write_kernel(states_ref, relaxed_ref, states_out, relaxed_out, held, in_sem, out_sem):
    layers = states_ref.shape[0]
    places = [(states_ref, states_out, l, l) for l in range(layers)]
    places.append((relaxed_ref, relaxed_out, 0, layers))
    reads, writes = [], []
    for src, dst, n, at in places:
        reads.append(pltpu.make_async_copy(src.at[n], held.at[at], in_sem.at[at]))
        writes.append(pltpu.make_async_copy(held.at[at], dst.at[n], out_sem.at[at]))
    for copy in reads:
        copy.start()
    for read, write in zip(reads, writes):
        read.wait()
        write.start()
    for copy in writes:
        copy.wait()


def shards(depths, spaces, coarse_states, first_kernels, second_kernels, coarse_channel_gain):
    layers, taps, chans, _ = first_kernels.shape
    _, rows, cols, _ = coarse_states.shape
    assert rows == 2 * layers and layers == 4 and spaces % 2 == 0 and depths % 2 == 0
    wide = column_windows(cols)[0][1]
    hbm = pl.BlockSpec(memory_space=pltpu.HBM)
    field = pltpu.VMEM((rows, cols, chans), BF16)
    slabs = pltpu.VMEM((3, 2, rows, wide, chans), BF16)
    few = pltpu.VMEM((3, 2, layers, wide, chans), BF16)
    mids = pltpu.VMEM((3, 2, layers, cols, chans), BF16)
    dma = pltpu.SemaphoreType.DMA
    results = (
        jax.ShapeDtypeStruct((layers, rows, cols, chans), F32),
        jax.ShapeDtypeStruct((1, rows, cols, chans), F32),
    )
    states, relaxed = pl.pallas_call(
        functools.partial(cycle_kernel, depths, spaces),
        out_shape=results,
        in_specs=[hbm] * 4,
        out_specs=(hbm, hbm),
        scratch_shapes=[
            pltpu.VMEM((layers, taps, chans, chans), BF16),
            pltpu.VMEM((layers, taps, chans, chans), BF16),
            pltpu.VMEM(coarse_channel_gain.shape, F32),
            pltpu.VMEM((2 * layers, 3 * rows, 3, cols, chans), BF16),
            pltpu.VMEM((layers + 1, 3 * rows, cols, chans), F32),
            slabs,
            few,
            mids,
            pltpu.VMEM((2, layers, cols, chans), BF16),
            slabs,
            pltpu.VMEM((2, rows, wide, chans), BF16),
            field,
            field,
            field,
            field,
            dma((rows,)),
            dma((2, layers)),
            dma,
            dma((3, 2)),
            dma((3, 2)),
            dma((3, 2)),
            dma((3, 2)),
            dma((3, 2, 2)),
            dma((3, 2, 2)),
            dma((2, 2)),
            dma((2, 2)),
            dma((2, rows, 2)),
            dma((2, rows, 2)),
            dma((layers, rows)),
            dma((rows,)),
        ],
        compiler_params=pltpu.CompilerParams(
            collective_id=0, has_side_effects=True, vmem_limit_bytes=58 * 1024 * 1024
        ),
    )(coarse_states[0], first_kernels, second_kernels, coarse_channel_gain)
    return pl.pallas_call(
        write_kernel,
        out_shape=results,
        in_specs=[hbm] * 2,
        out_specs=(hbm, hbm),
        scratch_shapes=[
            pltpu.VMEM((layers + 1, rows, cols, chans), F32),
            dma((layers + 1,)),
            dma((layers + 1,)),
        ],
    )(states, relaxed)


def solution(mesh):
    depths, spaces = mesh.shape["depth"], mesh.shape["space"]
    placed = (
        P("depth", "space", None, None),
        P("depth", None, None, None),
        P("depth", None, None, None),
        P(),
    )
    return jax.shard_map(
        functools.partial(shards, depths, spaces),
        mesh=mesh,
        in_specs=placed,
        out_specs=(P("depth", "space", None, None), P("depth", "space", None, None)),
        check_vma=False,
    )
```
